256 devices in a mesh: row: 32 (over z_lo, x, core), col: 8 (over z_hi, y).
Axes of the slice: x: 4, y: 4, z: 8 (z_hi: 2, z_lo: 4; z = z_hi * 4 + z_lo), core: 2. Of those that a mesh axis runs over, the one named last changes fastest.
Arguments:
- activations: bfloat16 [1024, 16384], P('col', 'row'), may hold values from 0 to 2
- blocks_one: bfloat16 [32, 8, 64, 128, 128], P('row', 'col'), may hold values from -0.09375 to 0.09375
- pattern_one: int32 [32, 8, 64], P('row', 'col'), may hold values from 0 to 63, as said below
- count_one: int32 [32, 8], P('row', 'col'), may hold values from 1 to 64, as said below
- blocks_two: bfloat16 [8, 32, 64, 128, 128], P('col', 'row'), may hold values from -0.125 to 0.125
- pattern_two: int32 [8, 32, 64], P('col', 'row'), may hold values from 0 to 63, as said below
- count_two: int32 [8, 32], P('col', 'row'), may hold values from 1 to 64, as said below
Outputs:
- sparse_out: bfloat16 [1024, 16384], P('col', 'row')
The draws below stay inside these ranges and needn't reach their ends.
Inputs may be any that keep to these rules, and one draw needn't show every extreme that they name: `pattern_one`: in each tile the slots below its count hold distinct positions; slots at or above the count hold positions in range whose blocks are not part of the weights. `count_one`: some tile has exactly 64 live slots. `pattern_two`: in each tile the slots below its count hold distinct positions; slots at or above the count hold positions in range whose blocks are not part of the weights. `count_two`: some tile has exactly 64 live slots.
All inputs are finite; a program needn't handle non-finite values.
Results may differ from the reference program's by a relative error of at most 0.0053.
Values may be sent and summed in bfloat16 or wider, within the bound.
A program may use at most 64 MiB of HBM per device.

```python
import jax
import jax.numpy as jnp
from jax import lax

N = 16384
BLK = 128
MAXB = 64
ROWS = 1024
BC_ONE = 16
BC_TWO = 4
TILE_SLOTS = 64
N_ROW = 32
N_COL = 8


def make_pattern(key, tiles):
    key_first = jax.random.fold_in(key, 11)
    key_second = jax.random.fold_in(key, 12)
    key_top = jax.random.fold_in(key, 13)
    key_place = jax.random.fold_in(key, 14)
    first = jax.random.randint(key_first, (tiles,), 0, MAXB)
    second = jax.random.randint(key_second, (tiles,), 0, MAXB)
    counts = 1 + first * second // MAXB
    top = jax.random.randint(key_top, (), 0, tiles)
    counts = jnp.where(jnp.arange(tiles) == top, MAXB, counts).astype(jnp.int32)
    keys = jax.random.split(key_place, tiles)
    places = jax.vmap(lambda k: jax.random.permutation(k, TILE_SLOTS)[:MAXB])(keys).astype(jnp.int32)
    return (places, counts)


def draw_pattern_one(key, part):
    places, counts = make_pattern(jax.random.fold_in(key, 1), N_ROW * N_COL)
    return places.reshape(N_ROW, N_COL, MAXB)


def draw_count_one(key, part):
    places, counts = make_pattern(jax.random.fold_in(key, 1), N_ROW * N_COL)
    return counts.reshape(N_ROW, N_COL)


def draw_pattern_two(key, part):
    places, counts = make_pattern(jax.random.fold_in(key, 2), N_COL * N_ROW)
    return places.reshape(N_COL, N_ROW, MAXB)


def draw_count_two(key, part):
    places, counts = make_pattern(jax.random.fold_in(key, 2), N_COL * N_ROW)
    return counts.reshape(N_COL, N_ROW)


def block_scale(rng, dims, cuts, smallest, largest):
    loudness = 1.0
    for dim, shards_of in cuts:
        steps = jax.random.uniform(jax.random.fold_in(jax.random.fold_in(rng, 6), dim), (shards_of,), jnp.float32, smallest / len(cuts), largest / len(cuts))
        loudness = loudness * jnp.repeat(jnp.exp(steps), dims[dim] // shards_of).reshape((-1,) + (1,) * (len(dims) - 1 - dim))
    return loudness


def normal_values(stream_key, extent, deviation, bound, cuts=(), held_as=jnp.bfloat16):
    entries = deviation * jax.random.normal(stream_key, extent, jnp.float32)
    if cuts:
        entries = entries * block_scale(stream_key, extent, cuts, -0.22, 0.18)
    return jnp.clip(entries, -bound, bound).astype(held_as)


def setup_inputs(seed: int = 0) -> dict:
    key_list = jax.random.split(jax.random.key(seed), 8)
    return {
        "activations": jnp.clip(2.0 * jax.random.uniform(key_list[0], (ROWS, N), jnp.float32) ** block_scale(key_list[0], (ROWS, N), ((0, 8), (1, 32)), -0.2, 0.2), 0.0, 2.0).astype(jnp.bfloat16),
        "blocks_one": normal_values(key_list[1], (N_ROW, N_COL, MAXB, BLK, BLK), (BLK * max(1, N_ROW * MAXB // (4 * BC_ONE))) ** -0.5, 0.09375, ((0, 32), (1, 8))),
        "pattern_one": draw_pattern_one(jax.random.fold_in(key_list[7], 71), 0),
        "count_one": draw_count_one(jax.random.fold_in(key_list[7], 71), 0),
        "blocks_two": normal_values(key_list[4], (N_COL, N_ROW, MAXB, BLK, BLK), (BLK * max(1, N_COL * MAXB // (8 * BC_TWO))) ** -0.5, 0.125, ((0, 8), (1, 32))),
        "pattern_two": draw_pattern_two(jax.random.fold_in(key_list[7], 71), 0),
        "count_two": draw_count_two(jax.random.fold_in(key_list[7], 71), 0),
    }


bias_value = -0.3


def dense_tile(where, live, blocks, block_rows, block_cols):
    slots = blocks.shape[0]
    size = blocks.shape[-1]
    places = jnp.arange(block_rows * block_cols, dtype=jnp.int32)
    used = jnp.arange(slots, dtype=jnp.int32) < live
    onehot = ((where[:, None] == places[None, :]) & used[:, None]).astype(jnp.float32)
    tiles = jnp.einsum("st,sab->tab", onehot, blocks.astype(jnp.float32), precision=lax.Precision.HIGHEST)
    tiles = tiles.reshape(block_rows, block_cols, size, size).transpose(0, 2, 1, 3)
    return tiles.reshape(block_rows * size, block_cols * size)


def layer(act, where, live, blocks, parts_in, parts_out):
    size = blocks.shape[-1]
    in_width = N // parts_in
    out_width = N // parts_out
    block_rows = in_width // size
    block_cols = out_width // size

    def column(b):
        def add(acc, a):
            tile = dense_tile(where[a, b], live[a, b], blocks[a, b], block_rows, block_cols)
            left = lax.dynamic_slice_in_dim(act, a * in_width, in_width, 1).astype(jnp.float32)
            return acc + jnp.dot(left, tile, precision=lax.Precision.HIGHEST), None

        acc, _ = lax.scan(add, jnp.zeros((act.shape[0], out_width), jnp.float32), jnp.arange(parts_in, dtype=jnp.int32))
        return jnp.maximum(acc + bias_value, 0.0).astype(jnp.bfloat16)

    outs = lax.map(column, jnp.arange(parts_out, dtype=jnp.int32))
    return outs.transpose(1, 0, 2).reshape(act.shape[0], N)


def reference(activations, blocks_one, pattern_one, count_one, blocks_two, pattern_two, count_two):
    hidden = layer(activations, pattern_one, count_one, blocks_one, N_ROW, N_COL)
    return layer(hidden, pattern_two, count_two, blocks_two, N_COL, N_ROW)
```

```python
import jax
import jax.numpy as jnp
from jax import lax
from jax.experimental import pallas as pl
from jax.experimental.pallas import tpu as pltpu
from jax.sharding import PartitionSpec as P

MESH = pl.DeviceIdType.MESH
BIAS = -0.3
BLK = 128
SLOTS = 64
ROWS = 128
WIDE = 2048
NARROW = 512
CHUNKS = 8
HALF, PIECE = ROWS // 2, ROWS // 8
ORDER = ((0, 1), (0, 3), (1, 0), (1, 1), (1, 3), (1, 2), (0, 2), (0, 0))
AT = {step: k for k, step in enumerate(ORDER)}
LAST_OTHER = max(AT[1, d] for d in range(4))
PLAN = (
    ("spread_core", 4),
    ("first", 0),
    ("sum_x", 1),
    ("second", 4),
    ("sum_core", 0),
    ("sum_z", 2),
    ("spread_x", 3),
    ("sum_other", 5),
)
Z_TYPE = jnp.bfloat16


def kernel(
    table, act, blocks_one, blocks_two, out,
    stored_one, stored_two, tile_one, tile_two, rows_in, part_one, core_in, x_out, x_in, x_own, z_sum, z_out, z_in, hidden,
    part_two, kept, y_out, y_in, zh_out, zh_in,
    load_sem, act_send, act_recv, core_send, core_recv, x_send, x_recv, z_send, z_recv,
    hz_send, hz_recv, hx_send, hx_recv, hc_send, hc_recv, y_send, y_recv, zh_send, zh_recv,
):
    row, col = lax.axis_index("row"), lax.axis_index("col")
    zl, x, core = row // 8, (row // 2) % 4, row % 2
    zh, y = col // 4, col % 4

    def row_at(zl, x, core):
        return ((zl * 4 + x) * 2 + core, col)

    other_core = row_at(zl, x, 1 - core)
    x_peer = [row_at(zl, (x + d) % 4, core) for d in range(4)]
    z_peer = [row_at((zl + d) % 4, x, core) for d in range(4)]
    y_peer = [(row, zh * 4 + (y + d) % 4) for d in range(4)]
    zh_peer = (row, (1 - zh) * 4 + y)

    def send(src, dst, send_sem, recv_sem, device):
        return pltpu.make_async_remote_copy(
            src_ref=src, dst_ref=dst, send_sem=send_sem, recv_sem=recv_sem,
            device_id=device, device_id_type=MESH,
        )

    def act_copy(src, k, device):
        return send(src, rows_in.at[k], act_send.at[k], act_recv.at[k], device)

    def core_copy(k):
        src = part_one.at[k, pl.ds(pl.multiple_of((1 - core) * HALF, HALF), HALF)]
        return send(src, core_in.at[k], core_send.at[k], core_recv.at[k], other_core)

    def x_copy(k, d):
        src = x_out.at[k, pl.ds(pl.multiple_of((x + d) % 4 * PIECE, PIECE), PIECE)]
        return send(src, x_in.at[k, d - 1], x_send.at[k, d - 1], x_recv.at[k, d - 1], x_peer[d])

    def z_copy(k, d):
        src = z_out.at[k, :, pl.ds(pl.multiple_of((zl + d) % 4 * NARROW, NARROW), NARROW)]
        return send(src, z_in.at[k, d - 1], z_send.at[k, d - 1], z_recv.at[k, d - 1], z_peer[d])

    mine = pl.ds(pl.multiple_of(core * HALF + x * PIECE, PIECE), PIECE)
    my_half = pl.ds(pl.multiple_of(core * HALF, HALF), HALF)
    my_cols = pl.ds(pl.multiple_of(zl * NARROW, NARROW), NARROW)

    def hz_copy(k, d):
        ref = hidden.at[k, mine, my_cols]
        return send(ref, ref, hz_send.at[k, d - 1], hz_recv.at[k, d - 1], z_peer[d])

    def hx_copy(k, d):
        ref = hidden.at[k, mine]
        return send(ref, ref, hx_send.at[k, d - 1], hx_recv.at[k, d - 1], x_peer[d])

    def hc_copy(k):
        ref = hidden.at[k, my_half]
        return send(ref, ref, hc_send.at[k], hc_recv.at[k], other_core)

    def y_copy(half, d):
        return send(
            y_out.at[half, d - 1], y_in.at[half, d - 1], y_send.at[half, d - 1], y_recv.at[half, d - 1], y_peer[d]
        )

    def zh_copy():
        return send(zh_out, zh_in, zh_send, zh_recv, zh_peer)

    def act_sends():
        yield act_copy(act, AT[1, 0], zh_peer)
        for d in (3, 1, 2):
            yield act_copy(act, AT[0, 4 - d], y_peer[d])

    def act_forwards():
        for d in (3, 1, 2):
            yield act_copy(rows_in.at[AT[1, 0]], AT[1, 4 - d], y_peer[d])

    loads = [
        pltpu.make_async_copy(ref, stored.at[pl.ds(0, SLOTS)], load_sem.at[layer])
        for layer, (ref, stored) in enumerate(((blocks_one, stored_one), (blocks_two, stored_two)))
    ]
    for load in loads:
        load.start()

    barrier = pltpu.get_barrier_semaphore()
    partners = [other_core, zh_peer, *x_peer[1:], *z_peer[1:], *y_peer[1:]]
    for device in partners:
        pl.semaphore_signal(barrier, inc=1, device_id=device, device_id_type=MESH)
    pl.semaphore_wait(barrier, len(partners))

    for copy in act_sends():
        copy.start()
    rows_in[AT[0, 0]] = act[...]
    for stored in (stored_one, stored_two):
        stored[SLOTS] = jnp.zeros((BLK, BLK), jnp.bfloat16)

    def build(layer, stored, tile, block_cols):
        def place(p, _):
            r = pl.multiple_of(p // block_cols * BLK, BLK)
            c = pl.multiple_of(p % block_cols * BLK, BLK)
            tile[pl.ds(r, BLK), pl.ds(c, BLK)] = stored[table[layer, p]]
            return 0

        loads[layer].wait()
        lax.fori_loop(0, SLOTS, place, 0)

    build(0, stored_one, tile_one, WIDE // BLK)

    def first(k):
        @pl.when(k != AT[0, 0])
        def _():
            act_copy(act, k, zh_peer).wait_recv()

        @pl.when(k == AT[1, 0])
        def _():
            for copy in act_forwards():
                copy.start()

        for n in range(WIDE // NARROW):
            cols = pl.ds(n * NARROW, NARROW)
            part_one[k, :, cols] = jnp.dot(rows_in[k], tile_one[:, cols], preferred_element_type=jnp.float32)
        core_copy(k).start()

    def sum_core(k):
        core_copy(k).wait_recv()
        x_out[k] = (part_one[k, my_half] + core_in[k]).astype(jnp.bfloat16)
        for d in (1, 3, 2):
            x_copy(k, d).start()
        x_own[k] = part_one[k, mine] + core_in[k, pl.ds(pl.multiple_of(x * PIECE, PIECE), PIECE)]

    def sum_x(k):
        for d in (1, 3, 2):
            x_copy(k, d).wait_recv()
        total = x_own[k]
        for d in range(3):
            total += x_in[k, d].astype(jnp.float32)
        z_out[k] = total.astype(z_out.dtype)
        for d in (1, 3, 2):
            z_copy(k, d).start()
        z_sum[k] = total

    def sum_z(k):
        for d in (1, 3, 2):
            z_copy(k, d).wait_recv()
        total = z_sum[k, :, my_cols]
        for d in range(3):
            total += z_in[k, d].astype(jnp.float32)
        hidden[k, mine, my_cols] = jnp.maximum(total + BIAS, 0.0).astype(jnp.bfloat16)
        for d in (1, 3, 2):
            hz_copy(k, d).start()

    def spread_x(k):
        for d in (1, 3, 2):
            hz_copy(k, d).wait_recv()
        for d in (1, 3, 2):
            hx_copy(k, d).start()

    def spread_core(k):
        for d in (1, 3, 2):
            hx_copy(k, d).wait_recv()
        hc_copy(k).start()

    def second(k):
        @pl.when(k == 0)
        def _():
            build(1, stored_two, tile_two, NARROW // BLK)

        hc_copy(k).wait_recv()
        part_two[...] = jnp.dot(hidden[k], tile_two[...], preferred_element_type=jnp.float32)
        for step, (half, d) in enumerate(ORDER):

            @pl.when(k == step)
            def _():
                if d:
                    y_out[half, d - 1] = part_two[...].astype(jnp.bfloat16)
                    y_copy(half, d).start()
                else:
                    kept[half] = part_two[...]

    def share_sum(half):
        total = kept[half]
        for d in range(3):
            total += y_in[half, d].astype(jnp.float32)
        return total

    def sum_other(k):
        @pl.when(k == LAST_OTHER)
        def _():
            for d in (1, 3, 2):
                y_copy(1, d).wait_recv()
            zh_out[...] = share_sum(1).astype(zh_out.dtype)
            zh_copy().start()

    stages = dict(
        first=first, sum_core=sum_core, sum_x=sum_x, sum_z=sum_z,
        spread_x=spread_x, spread_core=spread_core, second=second, sum_other=sum_other,
    )

    def step(t, _):
        for name, lag in PLAN:
            k = t - lag

            @pl.when((k >= 0) & (k < CHUNKS))
            def _():
                stages[name](k)

        return 0

    lax.fori_loop(0, CHUNKS + max(lag for _, lag in PLAN), step, 0)

    for d in (1, 3, 2):
        y_copy(0, d).wait_recv()
    zh_copy().wait_recv()
    total = share_sum(0) + zh_in[...].astype(jnp.float32)
    out[...] = jnp.maximum(total + BIAS, 0.0).astype(jnp.bfloat16)

    def sent(k, _):
        core_copy(k).wait_send()
        hc_copy(k).wait_send()
        for d in (1, 2, 3):
            x_copy(k, d).wait_send()
            z_copy(k, d).wait_send()
            hz_copy(k, d).wait_send()
            hx_copy(k, d).wait_send()
        return 0

    lax.fori_loop(0, CHUNKS, sent, 0)
    for copy in (*act_sends(), *act_forwards(), *(y_copy(half, d) for half in (0, 1) for d in (1, 2, 3)), zh_copy()):
        copy.wait_send()


def fused(table, act, blocks_one, blocks_two):
    bf16, f32 = jnp.bfloat16, jnp.float32
    dma = pltpu.SemaphoreType.DMA
    whole = pl.BlockSpec(memory_space=pltpu.VMEM)
    apart = pl.BlockSpec(memory_space=pl.ANY)
    scratch = [
        pltpu.VMEM((SLOTS + 1, BLK, BLK), bf16),
        pltpu.VMEM((SLOTS + 1, BLK, BLK), bf16),
        pltpu.VMEM((NARROW, WIDE), bf16),
        pltpu.VMEM((WIDE, NARROW), bf16),
        pltpu.VMEM((CHUNKS, ROWS, NARROW), bf16),
        pltpu.VMEM((CHUNKS, ROWS, WIDE), f32),
        pltpu.VMEM((CHUNKS, HALF, WIDE), f32),
        pltpu.VMEM((CHUNKS, HALF, WIDE), bf16),
        pltpu.VMEM((CHUNKS, 3, PIECE, WIDE), bf16),
        pltpu.VMEM((CHUNKS, PIECE, WIDE), f32),
        pltpu.VMEM((CHUNKS, PIECE, WIDE), f32),
        pltpu.VMEM((CHUNKS, PIECE, WIDE), Z_TYPE),
        pltpu.VMEM((CHUNKS, 3, PIECE, NARROW), Z_TYPE),
        pltpu.VMEM((CHUNKS, ROWS, WIDE), bf16),
        pltpu.VMEM((ROWS, NARROW), f32),
        pltpu.VMEM((2, ROWS, NARROW), f32),
        pltpu.VMEM((2, 3, ROWS, NARROW), bf16),
        pltpu.VMEM((2, 3, ROWS, NARROW), bf16),
        pltpu.VMEM((ROWS, NARROW), bf16),
        pltpu.VMEM((ROWS, NARROW), bf16),
        dma((2,)),
    ]
    for shape in ((CHUNKS,), (CHUNKS,), (CHUNKS, 3), (CHUNKS, 3), (CHUNKS, 3), (CHUNKS, 3), (CHUNKS,), (2, 3), ()):
        scratch += [dma(shape), dma(shape)]
    return pl.pallas_call(
        kernel,
        name="fused_layers",
        out_shape=jax.ShapeDtypeStruct((ROWS, NARROW), bf16),
        in_specs=[pl.BlockSpec(memory_space=pltpu.SMEM), whole, apart, apart],
        out_specs=whole,
        scratch_shapes=scratch,
        compiler_params=pltpu.CompilerParams(collective_id=0, has_side_effects=True, vmem_limit_bytes=56 << 20),
    )(table, act, blocks_one, blocks_two)


def slot_at(pattern, count):
    where, live = pattern.reshape(-1), count.reshape(())
    slots = jnp.arange(SLOTS, dtype=jnp.int32)
    hit = (slots[:, None] == where[None, :]) & (slots < live)[None, :]
    return jnp.min(jnp.where(hit, slots[None, :], SLOTS), axis=1)


def shards(activations, blocks_one, pattern_one, count_one, blocks_two, pattern_two, count_two):
    table = jnp.stack([slot_at(pattern_one, count_one), slot_at(pattern_two, count_two)])
    return fused(
        table, activations, blocks_one.reshape(SLOTS, BLK, BLK), blocks_two.reshape(SLOTS, BLK, BLK)
    )


def solution(mesh):
    return jax.shard_map(
        shards,
        mesh=mesh,
        in_specs=(
            P("col", "row"),
            P("row", "col", None, None, None),
            P("row", "col", None),
            P("row", "col"),
            P("col", "row", None, None, None),
            P("col", "row", None),
            P("col", "row"),
        ),
        out_specs=P("col", "row"),
        check_vma=False,
    )
```

```python
import jax
import jax.numpy as jnp
from jax import lax
from jax.experimental import pallas as pl
from jax.experimental.pallas import tpu as pltpu
from jax.sharding import PartitionSpec as P

MESH = pl.DeviceIdType.MESH
BIAS = -0.3
BLK = 128
SLOTS = 64
LANES = 128
ROWS = 128
WIDE = 2048
NARROW = 512
CHUNKS = 8
HALF, PIECE = ROWS // 2, ROWS // 8
ORDER = (
    (1, 2), (0, 3), (0, 0), (0, 1), (0, 2), (1, 0), (1, 1), (1, 3),
)
AT = {step: k for k, step in enumerate(ORDER)}
STAGES = (
    "first",
    "sum_core",
    "relay",
    "sum_x",
    "sum_z",
    "spread_x",
    "pass_x",
    "spread_core",
    "second",
    "sum_other",
    "build_two",
)
SCHEDULE = (
    2, 3, 10, 1, 11, 5, 9, 80, 19, 13, 17, 7, 6, 21, 18, 27,
    15, 0, 14, 4, 25, 23, 8, 35, 22, 29, 31, 16, 12, 43, 30, 24,
    39, 20, 38, 32, 28, 51, 47, 46, 33, 40, 37, 26, 55, 54, 59, 36,
    48, 41, 63, 62, 45, 71, 70, 56, 44, 34, 53, 49, 64, 52, 67, 61,
    57, 60, 69, 72, 42, 68, 50, 65, 58, 66,
)
STEP = (1, 3)
SIDE = (pl.ds(0, WIDE // 2), pl.ds(WIDE // 2, WIDE // 2))
Z_TYPE = jnp.bfloat16


PACK, CODES = 4, 128
IDLE = CODES - 1
WORDS = []
for _start in range(0, len(SCHEDULE), PACK):
    _codes = (SCHEDULE[_start : _start + PACK] + (IDLE,) * PACK)[:PACK]
    WORDS.append(sum(code * CODES**n for n, code in enumerate(_codes)))


def kernel(
    act, blocks_one, pattern_one, count_one, blocks_two, pattern_two, count_two, out,
    stored_one, stored_two, tile_one, tile_two, rows_in, part_one, core_in, x_out, far_in, near_in, relay_out, relay_in, z_sum, z_out, z_in, hidden,
    part_two, kept, y_out, y_in, zh_out, zh_in,
    found, table, load_sem, act_send, act_recv, core_send, core_recv, far_send, far_recv, near_send, near_recv, relay_send, relay_recv, z_send, z_recv,
    hz_send, hz_recv, hx_send, hx_recv, pass_send, pass_recv, hc_send, hc_recv, y_send, y_recv, zh_send, zh_recv,
):
    row, col = lax.axis_index("row"), lax.axis_index("col")
    zl, x, core = row // 8, (row // 2) % 4, row % 2
    zh, y = col // 4, col % 4

    def row_at(zl, x, core):
        return ((zl * 4 + x) * 2 + core, col)

    other_core = row_at(zl, x, 1 - core)
    x_peer = [row_at(zl, (x + d) % 4, core) for d in range(4)]
    z_peer = [row_at((zl + d) % 4, x, core) for d in range(4)]
    y_peer = [(row, zh * 4 + (y + d) % 4) for d in range(4)]
    zh_peer = (row, (1 - zh) * 4 + y)

    def send(src, dst, send_sem, recv_sem, device):
        return pltpu.make_async_remote_copy(
            src_ref=src, dst_ref=dst, send_sem=send_sem, recv_sem=recv_sem,
            device_id=device, device_id_type=MESH,
        )

    def act_copy(src, k, device):
        return send(src, rows_in.at[k], act_send.at[k], act_recv.at[k], device)

    def core_copy(k):
        src = part_one.at[k, pl.ds(pl.multiple_of((1 - core) * HALF, HALF), HALF)]
        return send(src, core_in.at[k], core_send.at[k], core_recv.at[k], other_core)

    def rows_of(step):
        return pl.ds(pl.multiple_of((x + step) % 4 * PIECE, PIECE), PIECE)

    def far_copy(k, way):
        src = x_out.at[k, rows_of(2), SIDE[way]]
        return send(src, far_in.at[k, way], far_send.at[k, way], far_recv.at[k, way], x_peer[STEP[way]])

    def near_copy(k, way):
        src = x_out.at[k, rows_of(STEP[way]), SIDE[1 - way]]
        return send(src, near_in.at[k, way], near_send.at[k, way], near_recv.at[k, way], x_peer[STEP[way]])

    def relay_copy(k, way):
        src = relay_out.at[k, way]
        return send(src, relay_in.at[k, way], relay_send.at[k, way], relay_recv.at[k, way], x_peer[STEP[way]])

    def z_copy(k, d):
        src = z_out.at[k, :, pl.ds(pl.multiple_of((zl + d) % 4 * NARROW, NARROW), NARROW)]
        return send(src, z_in.at[k, d - 1], z_send.at[k, d - 1], z_recv.at[k, d - 1], z_peer[d])

    mine = pl.ds(pl.multiple_of(core * HALF + x * PIECE, PIECE), PIECE)
    my_half = pl.ds(pl.multiple_of(core * HALF, HALF), HALF)
    my_cols = pl.ds(pl.multiple_of(zl * NARROW, NARROW), NARROW)

    def hz_copy(k, d):
        ref = hidden.at[k, mine, my_cols]
        return send(ref, ref, hz_send.at[k, d - 1], hz_recv.at[k, d - 1], z_peer[d])

    def hx_copy(k, way):
        ref = hidden.at[k, mine]
        return send(ref, ref, hx_send.at[k, way], hx_recv.at[k, way], x_peer[STEP[way]])

    def pass_copy(k, way):
        behind = core * HALF + (x + STEP[1 - way]) % 4 * PIECE
        ref = hidden.at[k, pl.ds(pl.multiple_of(behind, PIECE), PIECE), SIDE[way]]
        return send(ref, ref, pass_send.at[k, way], pass_recv.at[k, way], x_peer[STEP[way]])

    def hc_copy(k):
        ref = hidden.at[k, my_half]
        return send(ref, ref, hc_send.at[k], hc_recv.at[k], other_core)

    def y_copy(half, d):
        return send(
            y_out.at[half, d - 1], y_in.at[half, d - 1], y_send.at[half, d - 1], y_recv.at[half, d - 1], y_peer[d]
        )

    def zh_copy():
        return send(zh_out, zh_in, zh_send, zh_recv, zh_peer)

    def act_sends():
        yield act_copy(act, AT[0, 1], y_peer[3])
        yield act_copy(act, AT[1, 0], zh_peer)
        for d in (1, 2):
            yield act_copy(act, AT[0, 4 - d], y_peer[d])

    def act_forwards():
        for d in (3, 1, 2):
            yield act_copy(rows_in.at[AT[1, 0]], AT[1, 4 - d], y_peer[d])

    loads = [
        pltpu.make_async_copy(ref, stored.at[pl.ds(0, SLOTS)], load_sem.at[layer])
        for layer, (ref, stored) in enumerate(((blocks_one, stored_one), (blocks_two, stored_two)))
    ]
    for load in loads:
        load.start()

    place = lax.broadcasted_iota(jnp.int32, (LANES, LANES), 0)
    slot = lax.broadcasted_iota(jnp.int32, (LANES, LANES), 1)
    for layer, (pattern, count) in enumerate(((pattern_one, count_one), (pattern_two, count_two))):
        where = jnp.concatenate([pattern[...], jnp.zeros((1, LANES - SLOTS), jnp.int32)], axis=1)
        hit = (where == place) & (slot < count[0, 0])
        found[pl.ds(layer, 1), :] = jnp.min(jnp.where(hit, slot, SLOTS).T, axis=0, keepdims=True)
    fill = pltpu.make_async_copy(found, table, load_sem.at[2])
    fill.start()

    barrier = pltpu.get_barrier_semaphore()
    partners = [other_core, zh_peer, x_peer[1], x_peer[3], *z_peer[1:], *y_peer[1:]]
    for device in partners:
        pl.semaphore_signal(barrier, inc=1, device_id=device, device_id_type=MESH)
    pl.semaphore_wait(barrier, len(partners))

    for copy in act_sends():
        copy.start()
    rows_in[AT[0, 0]] = act[...]
    fill.wait()
    for stored in (stored_one, stored_two):
        stored[SLOTS] = jnp.zeros((BLK, BLK), jnp.bfloat16)

    def build(layer, stored, tile, block_cols):
        def put(p, _):
            r = pl.multiple_of(p // block_cols * BLK, BLK)
            c = pl.multiple_of(p % block_cols * BLK, BLK)
            tile[pl.ds(r, BLK), pl.ds(c, BLK)] = stored[table[layer, p]]
            return 0

        loads[layer].wait()
        lax.fori_loop(0, SLOTS, put, 0)

    build(0, stored_one, tile_one, WIDE // BLK)

    def first(k):
        @pl.when(k != AT[0, 0])
        def _():
            act_copy(act, k, zh_peer).wait_recv()

        @pl.when(k == AT[1, 0])
        def _():
            for copy in act_forwards():
                copy.start()

        for n in range(WIDE // NARROW):
            cols = pl.ds(n * NARROW, NARROW)
            part_one[k, :, cols] = jnp.dot(rows_in[k], tile_one[:, cols], preferred_element_type=jnp.float32)
        core_copy(k).start()

    def sum_core(k):
        core_copy(k).wait_recv()
        x_out[k] = (part_one[k, my_half] + core_in[k]).astype(jnp.bfloat16)
        for way in range(2):
            far_copy(k, way).start()
        for way in range(2):
            near_copy(k, way).start()

    def own_sum(k, step, cols):
        rows = core * HALF + (x + step) % 4 * PIECE
        return part_one[k, pl.ds(pl.multiple_of(rows, PIECE), PIECE), cols] + core_in[k, rows_of(step), cols]

    def relay(k):
        for way in range(2):
            far_copy(k, way).wait_recv()
            total = own_sum(k, STEP[way], SIDE[way]) + far_in[k, way].astype(jnp.float32)
            relay_out[k, way] = total.astype(jnp.bfloat16)
            relay_copy(k, way).start()

    def sum_x(k):
        for way in range(2):
            near_copy(k, way).wait_recv()
            relay_copy(k, way).wait_recv()
        sides = []
        for way in range(2):
            side = own_sum(k, 0, SIDE[way])
            side += near_in[k, 1 - way].astype(jnp.float32) + relay_in[k, way].astype(jnp.float32)
            sides.append(side)
        total = jnp.concatenate(sides, axis=1)
        z_out[k] = total.astype(z_out.dtype)
        for d in (1, 3, 2):
            z_copy(k, d).start()
        z_sum[k] = total

    def sum_z(k):
        for d in (1, 3, 2):
            z_copy(k, d).wait_recv()
        total = z_sum[k, :, my_cols]
        for d in range(3):
            total += z_in[k, d].astype(jnp.float32)
        hidden[k, mine, my_cols] = jnp.maximum(total + BIAS, 0.0).astype(jnp.bfloat16)
        for d in (1, 3, 2):
            hz_copy(k, d).start()

    def spread_x(k):
        for d in (1, 3, 2):
            hz_copy(k, d).wait_recv()
        for way in range(2):
            hx_copy(k, way).start()

    def pass_x(k):
        for way in range(2):
            hx_copy(k, way).wait_recv()
            pass_copy(k, way).start()

    def spread_core(k):
        for way in range(2):
            pass_copy(k, way).wait_recv()
        hc_copy(k).start()

    def second(k):
        hc_copy(k).wait_recv()
        part_two[...] = jnp.dot(hidden[k], tile_two[...], preferred_element_type=jnp.float32)
        for step, (half, d) in enumerate(ORDER):

            @pl.when(k == step)
            def _():
                if d:
                    y_out[half, d - 1] = part_two[...].astype(jnp.bfloat16)
                    y_copy(half, d).start()
                else:
                    kept[half] = part_two[...]

    def share_sum(half):
        total = kept[half]
        for d in range(3):
            total += y_in[half, d].astype(jnp.float32)
        return total

    def sum_other(k):
        for d in (1, 3, 2):
            y_copy(1, d).wait_recv()
        zh_out[...] = share_sum(1).astype(zh_out.dtype)
        zh_copy().start()

    def build_two(k):
        build(1, stored_two, tile_two, NARROW // BLK)

    here = locals()
    stages = [here[name] for name in STAGES]

    def group(n, _):
        word = jnp.int32(WORDS[0])
        for m in range(1, len(WORDS)):
            word = jnp.where(n == m, WORDS[m], word)

        def entry(_, word):
            code = lax.rem(word, CODES)
            for number, stage in enumerate(stages):

                @pl.when(lax.div(code, CHUNKS) == number)
                def _():
                    stage(lax.rem(code, CHUNKS))

            return lax.div(word, CODES)

        lax.fori_loop(0, PACK, entry, word)
        return 0

    lax.fori_loop(0, len(WORDS), group, 0)

    for d in (1, 3, 2):
        y_copy(0, d).wait_recv()
    zh_copy().wait_recv()
    out[...] = share_sum(0) + zh_in[...].astype(jnp.float32)

    def sent(k, _):
        core_copy(k).wait_send()
        hc_copy(k).wait_send()
        for way in range(2):
            for copy in (far_copy, near_copy, relay_copy, hx_copy, pass_copy):
                copy(k, way).wait_send()
        for d in (1, 2, 3):
            z_copy(k, d).wait_send()
            hz_copy(k, d).wait_send()
        return 0

    lax.fori_loop(0, CHUNKS, sent, 0)
    for copy in (*act_sends(), *act_forwards(), *(y_copy(half, d) for half in (0, 1) for d in (1, 2, 3)), zh_copy()):
        copy.wait_send()


def fused(act, blocks_one, pattern_one, count_one, blocks_two, pattern_two, count_two):
    bf16, f32 = jnp.bfloat16, jnp.float32
    dma = pltpu.SemaphoreType.DMA
    whole = pl.BlockSpec(memory_space=pltpu.VMEM)
    scalar = pl.BlockSpec(memory_space=pltpu.SMEM)
    apart = pl.BlockSpec(memory_space=pl.ANY)
    scratch = [
        pltpu.VMEM((SLOTS + 1, BLK, BLK), bf16),
        pltpu.VMEM((SLOTS + 1, BLK, BLK), bf16),
        pltpu.VMEM((NARROW, WIDE), bf16),
        pltpu.VMEM((WIDE, NARROW), bf16),
        pltpu.VMEM((CHUNKS, ROWS, NARROW), bf16),
        pltpu.VMEM((CHUNKS, ROWS, WIDE), f32),
        pltpu.VMEM((CHUNKS, HALF, WIDE), f32),
        pltpu.VMEM((CHUNKS, HALF, WIDE), bf16),
        pltpu.VMEM((CHUNKS, 2, PIECE, WIDE // 2), bf16),
        pltpu.VMEM((CHUNKS, 2, PIECE, WIDE // 2), bf16),
        pltpu.VMEM((CHUNKS, 2, PIECE, WIDE // 2), bf16),
        pltpu.VMEM((CHUNKS, 2, PIECE, WIDE // 2), bf16),
        pltpu.VMEM((CHUNKS, PIECE, WIDE), f32),
        pltpu.VMEM((CHUNKS, PIECE, WIDE), Z_TYPE),
        pltpu.VMEM((CHUNKS, 3, PIECE, NARROW), Z_TYPE),
        pltpu.VMEM((CHUNKS, ROWS, WIDE), bf16),
        pltpu.VMEM((ROWS, NARROW), f32),
        pltpu.VMEM((2, ROWS, NARROW), f32),
        pltpu.VMEM((2, 3, ROWS, NARROW), bf16),
        pltpu.VMEM((2, 3, ROWS, NARROW), bf16),
        pltpu.VMEM((ROWS, NARROW), bf16),
        pltpu.VMEM((ROWS, NARROW), bf16),
        pltpu.VMEM((2, LANES), jnp.int32),
        pltpu.SMEM((2, LANES), jnp.int32),
        dma((3,)),
    ]
    one, two, three = (CHUNKS,), (CHUNKS, 2), (CHUNKS, 3)
    for shape in (one, one, two, two, two, three, three, two, two, one, (2, 3), ()):
        scratch += [dma(shape), dma(shape)]
    return pl.pallas_call(
        kernel,
        name="fused_layers",
        out_shape=jax.ShapeDtypeStruct((ROWS, NARROW), f32),
        in_specs=[whole, apart, whole, scalar, apart, whole, scalar],
        out_specs=whole,
        scratch_shapes=scratch,
        compiler_params=pltpu.CompilerParams(collective_id=0, has_side_effects=True, vmem_limit_bytes=56 << 20),
    )(act, blocks_one, pattern_one, count_one, blocks_two, pattern_two, count_two)


def shards(activations, blocks_one, pattern_one, count_one, blocks_two, pattern_two, count_two):
    total = fused(
        activations,
        blocks_one.reshape(SLOTS, BLK, BLK),
        pattern_one.reshape(1, SLOTS),
        count_one,
        blocks_two.reshape(SLOTS, BLK, BLK),
        pattern_two.reshape(1, SLOTS),
        count_two,
    )
    return jnp.maximum(total + BIAS, 0.0).astype(jnp.bfloat16)


def solution(mesh):
    return jax.shard_map(
        shards,
        mesh=mesh,
        in_specs=(
            P("col", "row"),
            P("row", "col", None, None, None),
            P("row", "col", None),
            P("row", "col"),
            P("col", "row", None, None, None),
            P("col", "row", None),
            P("col", "row"),
        ),
        out_specs=P("col", "row"),
        check_vma=False,
    )
```

```python
import jax
import jax.numpy as jnp
from jax import lax
from jax.experimental import pallas as pl
from jax.experimental.pallas import tpu as pltpu
from jax.sharding import PartitionSpec as P

MESH = pl.DeviceIdType.MESH
BIAS = -0.3
BLK = 128
SLOTS = 64
LANES = 128
ROWS = 128
WIDE = 2048
NARROW = 512
CHUNKS = 8
HALF, PIECE = ROWS // 2, ROWS // 8
ORDER = (
    (0, 0), (1, 1), (1, 0), (0, 1), (0, 2), (1, 3), (1, 2), (0, 3),
)
AT = {step: k for k, step in enumerate(ORDER)}
STAGES = (
    "first",
    "sum_core",
    "relay",
    "sum_x",
    "sum_z",
    "spread_x",
    "pass_x",
    "spread_core",
    "second",
    "sum_other",
    "build_two",
    "forward",
)
SCHEDULE = (
    80, 0, 3, 88, 11, 4, 89, 8, 2, 19, 7, 12, 5, 10, 27, 6,
    13, 1, 18, 14, 21, 9, 35, 22, 26, 29, 17, 16, 43, 30, 34, 15,
    20, 25, 38, 51, 42, 37, 23, 33, 28, 46, 45, 31, 41, 54, 36, 50,
    53, 39, 49, 24, 62, 44, 58, 61, 70, 57, 47, 59, 69, 32, 52, 65,
    67, 55, 66, 40, 60, 72, 68, 73, 63, 48, 71, 56, 64,
)
STEP = (1, 3)
PART = (pl.ds(0, NARROW // 2), pl.ds(NARROW // 2, NARROW // 2))
SIDE = (pl.ds(0, WIDE // 2), pl.ds(WIDE // 2, WIDE // 2))
Z_TYPE = jnp.bfloat16


PACK, CODES = 4, 128
IDLE = CODES - 1
WORDS = []
for _start in range(0, len(SCHEDULE), PACK):
    _codes = (SCHEDULE[_start : _start + PACK] + (IDLE,) * PACK)[:PACK]
    WORDS.append(sum(code * CODES**n for n, code in enumerate(_codes)))


def kernel(
    act, blocks_one, pattern_one, count_one, blocks_two, pattern_two, count_two, out,
    patterns, counts,
    stored_one, stored_two, tile_one, tile_two, rows_in, part_one, core_in, x_out, far_in, near_in, relay_out, relay_in, z_sum, z_out, z_in, hidden,
    part_two, kept, y_out, y_in, zh_out, zh_in,
    found, table, load_sem, act_send, act_recv, core_send, core_recv, far_send, far_recv, near_send, near_recv, relay_send, relay_recv, z_send, z_recv,
    hz_send, hz_recv, hx_send, hx_recv, pass_send, pass_recv, hc_send, hc_recv, y_send, y_recv, zh_send, zh_recv,
):
    row, col = lax.axis_index("row"), lax.axis_index("col")
    zl, x, core = row // 8, (row // 2) % 4, row % 2
    zh, y = col // 4, col % 4

    def row_at(zl, x, core):
        return ((zl * 4 + x) * 2 + core, col)

    other_core = row_at(zl, x, 1 - core)
    x_peer = [row_at(zl, (x + d) % 4, core) for d in range(4)]
    z_peer = [row_at((zl + d) % 4, x, core) for d in range(4)]
    y_peer = [(row, zh * 4 + (y + d) % 4) for d in range(4)]
    zh_peer = (row, (1 - zh) * 4 + y)

    def send(src, dst, send_sem, recv_sem, device):
        return pltpu.make_async_remote_copy(
            src_ref=src, dst_ref=dst, send_sem=send_sem, recv_sem=recv_sem,
            device_id=device, device_id_type=MESH,
        )

    def act_copy(src, k, piece, device):
        rows = pl.ds(pl.multiple_of(piece * HALF, HALF), HALF)
        return send(src.at[rows], rows_in.at[k, rows], act_send.at[k, piece], act_recv.at[k, piece], device)

    def core_copy(k):
        src = part_one.at[k, pl.ds(pl.multiple_of((1 - core) * HALF, HALF), HALF)]
        return send(src, core_in.at[k], core_send.at[k], core_recv.at[k], other_core)

    def rows_of(step):
        return pl.ds(pl.multiple_of((x + step) % 4 * PIECE, PIECE), PIECE)

    def far_copy(k, way):
        src = x_out.at[k, rows_of(2), SIDE[way]]
        return send(src, far_in.at[k, way], far_send.at[k, way], far_recv.at[k, way], x_peer[STEP[way]])

    def near_copy(k, way):
        src = x_out.at[k, rows_of(STEP[way]), SIDE[1 - way]]
        return send(src, near_in.at[k, way], near_send.at[k, way], near_recv.at[k, way], x_peer[STEP[way]])

    def relay_copy(k, way):
        src = relay_out.at[k, way]
        return send(src, relay_in.at[k, way], relay_send.at[k, way], relay_recv.at[k, way], x_peer[STEP[way]])

    def z_copy(k, d):
        src = z_out.at[k, :, pl.ds(pl.multiple_of((zl + d) % 4 * NARROW, NARROW), NARROW)]
        return send(src, z_in.at[k, d - 1], z_send.at[k, d - 1], z_recv.at[k, d - 1], z_peer[d])

    mine = pl.ds(pl.multiple_of(core * HALF + x * PIECE, PIECE), PIECE)
    my_half = pl.ds(pl.multiple_of(core * HALF, HALF), HALF)
    my_cols = pl.ds(pl.multiple_of(zl * NARROW, NARROW), NARROW)

    def hz_copy(k, d):
        ref = hidden.at[k, mine, my_cols]
        return send(ref, ref, hz_send.at[k, d - 1], hz_recv.at[k, d - 1], z_peer[d])

    def hx_copy(k, way):
        ref = hidden.at[k, mine]
        return send(ref, ref, hx_send.at[k, way], hx_recv.at[k, way], x_peer[STEP[way]])

    def pass_copy(k, way):
        behind = core * HALF + (x + STEP[1 - way]) % 4 * PIECE
        ref = hidden.at[k, pl.ds(pl.multiple_of(behind, PIECE), PIECE), SIDE[way]]
        return send(ref, ref, pass_send.at[k, way], pass_recv.at[k, way], x_peer[STEP[way]])

    def hc_copy(k):
        ref = hidden.at[k, my_half]
        return send(ref, ref, hc_send.at[k], hc_recv.at[k], other_core)

    def y_copy(half, d, piece):
        at = (half, d - 1, piece)
        return send(y_out.at[at], y_in.at[at], y_send.at[at], y_recv.at[at], (row, zh * 4 + (y + d) % 4))

    def zh_copy(piece):
        return send(zh_out.at[piece], zh_in.at[piece], zh_send.at[piece], zh_recv.at[piece], zh_peer)

    def act_sends():
        for piece in range(2):
            yield act_copy(rows_in.at[AT[0, 0]], AT[1, 0], piece, zh_peer)
        for d in (3, 1, 2):
            for piece in range(2):
                yield act_copy(rows_in.at[AT[0, 0]], AT[0, 4 - d], piece, y_peer[d])

    def act_forwards(piece):
        for d in (3, 1, 2):
            yield act_copy(rows_in.at[AT[1, 0]], AT[1, 4 - d], piece, y_peer[d])

    barrier = pltpu.get_barrier_semaphore()
    partners = [other_core, zh_peer, x_peer[1], x_peer[3], *z_peer[1:], *y_peer[1:]]
    for device in partners:
        pl.semaphore_signal(barrier, inc=1, device_id=device, device_id_type=MESH)

    own = AT[0, 0]
    own_load = pltpu.make_async_copy(act, rows_in.at[own], load_sem.at[3])
    facts = [
        pltpu.make_async_copy(src, dst, load_sem.at[n])
        for n, (src, dst) in enumerate(
            (
                (pattern_one, patterns.at[0]),
                (pattern_two, patterns.at[1]),
                (count_one, counts.at[0]),
                (count_two, counts.at[1]),
            ),
            start=4,
        )
    ]
    loads = [
        pltpu.make_async_copy(ref, stored.at[pl.ds(0, SLOTS)], load_sem.at[layer])
        for layer, (ref, stored) in enumerate(((blocks_one, stored_one), (blocks_two, stored_two)))
    ]
    for load in (own_load, *facts, *loads):
        load.start()
    for stored in (stored_one, stored_two):
        stored[SLOTS] = jnp.zeros((BLK, BLK), jnp.bfloat16)
    for fact in facts:
        fact.wait()

    place = lax.broadcasted_iota(jnp.int32, (LANES, LANES), 0)
    slot = lax.broadcasted_iota(jnp.int32, (LANES, LANES), 1)
    for layer in range(2):
        where = jnp.concatenate([patterns[layer], jnp.zeros((1, LANES - SLOTS), jnp.int32)], axis=1)
        hit = (where == place) & (slot < counts[layer, 0, 0])
        found[pl.ds(layer, 1), :] = jnp.min(jnp.where(hit, slot, SLOTS).T, axis=0, keepdims=True)
    fill = pltpu.make_async_copy(found, table, load_sem.at[2])
    fill.start()
    own_load.wait()

    pl.semaphore_wait(barrier, len(partners))
    for copy in act_sends():
        copy.start()
    fill.wait()

    def build(layer, stored, tile, block_cols):
        def put(p, _):
            r = pl.multiple_of(p // block_cols * BLK, BLK)
            c = pl.multiple_of(p % block_cols * BLK, BLK)
            tile[pl.ds(r, BLK), pl.ds(c, BLK)] = stored[table[layer, p]]
            return 0

        loads[layer].wait()
        lax.fori_loop(0, SLOTS, put, 0)

    build(0, stored_one, tile_one, WIDE // BLK)

    def forward(piece):
        act_copy(rows_in.at[AT[0, 0]], AT[1, 0], piece, zh_peer).wait_recv()
        for copy in act_forwards(piece):
            copy.start()

    def first(k):
        @pl.when((k != AT[0, 0]) & (k != AT[1, 0]))
        def _():
            for piece in range(2):
                act_copy(rows_in.at[AT[0, 0]], k, piece, zh_peer).wait_recv()

        for n in range(WIDE // NARROW):
            cols = pl.ds(n * NARROW, NARROW)
            part_one[k, :, cols] = jnp.dot(rows_in[k], tile_one[:, cols], preferred_element_type=jnp.float32)
        core_copy(k).start()

    def sum_core(k):
        core_copy(k).wait_recv()
        x_out[k] = (part_one[k, my_half] + core_in[k]).astype(jnp.bfloat16)
        for way in range(2):
            far_copy(k, way).start()
        for way in range(2):
            near_copy(k, way).start()

    def own_sum(k, step, cols):
        rows = core * HALF + (x + step) % 4 * PIECE
        return part_one[k, pl.ds(pl.multiple_of(rows, PIECE), PIECE), cols] + core_in[k, rows_of(step), cols]

    def relay(k):
        for way in range(2):
            far_copy(k, way).wait_recv()
            total = own_sum(k, STEP[way], SIDE[way]) + far_in[k, way].astype(jnp.float32)
            relay_out[k, way] = total.astype(jnp.bfloat16)
            relay_copy(k, way).start()

    def sum_x(k):
        for way in range(2):
            near_copy(k, way).wait_recv()
            relay_copy(k, way).wait_recv()
        sides = []
        for way in range(2):
            side = own_sum(k, 0, SIDE[way])
            side += near_in[k, 1 - way].astype(jnp.float32) + relay_in[k, way].astype(jnp.float32)
            sides.append(side)
        total = jnp.concatenate(sides, axis=1)
        z_out[k] = total.astype(z_out.dtype)
        for d in (1, 3, 2):
            z_copy(k, d).start()
        z_sum[k] = total

    def sum_z(k):
        for d in (1, 3, 2):
            z_copy(k, d).wait_recv()
        total = z_sum[k, :, my_cols]
        for d in range(3):
            total += z_in[k, d].astype(jnp.float32)
        hidden[k, mine, my_cols] = jnp.maximum(total + BIAS, 0.0).astype(jnp.bfloat16)
        for d in (1, 3, 2):
            hz_copy(k, d).start()

    def spread_x(k):
        for d in (1, 3, 2):
            hz_copy(k, d).wait_recv()
        for way in range(2):
            hx_copy(k, way).start()

    def pass_x(k):
        for way in range(2):
            hx_copy(k, way).wait_recv()
            pass_copy(k, way).start()

    def spread_core(k):
        for way in range(2):
            pass_copy(k, way).wait_recv()
        hc_copy(k).start()

    def second(k):
        hc_copy(k).wait_recv()
        half, d = jnp.int32(ORDER[0][0]), jnp.int32(ORDER[0][1])
        for other, steps in enumerate(ORDER):
            half = jnp.where(k == other, steps[0], half)
            d = jnp.where(k == other, steps[1], d)
        for piece in range(2):
            part_two[...] = jnp.dot(hidden[k], tile_two[:, PART[piece]], preferred_element_type=jnp.float32)

            @pl.when(d == 0)
            def _():
                kept[half, piece] = part_two[...]

            @pl.when(d != 0)
            def _():
                y_out[half, d - 1, piece] = part_two[...].astype(jnp.bfloat16)
                y_copy(half, d, piece).start()

    def share_sum(half, piece):
        total = kept[half, piece]
        for d in range(3):
            total += y_in[half, d, piece].astype(jnp.float32)
        return total

    def sum_other(piece):
        for d in (1, 3, 2):
            y_copy(1, d, piece).wait_recv()
        zh_out[piece] = share_sum(1, piece).astype(zh_out.dtype)
        zh_copy(piece).start()

    def build_two(k):
        build(1, stored_two, tile_two, NARROW // BLK)

    here = locals()
    stages = [here[name] for name in STAGES]

    def group(n, _):
        word = jnp.int32(WORDS[0])
        for m in range(1, len(WORDS)):
            word = jnp.where(n == m, WORDS[m], word)

        def entry(_, word):
            code = lax.rem(word, CODES)
            for number, stage in enumerate(stages):

                @pl.when(lax.div(code, CHUNKS) == number)
                def _():
                    stage(lax.rem(code, CHUNKS))

            return lax.div(word, CODES)

        lax.fori_loop(0, PACK, entry, word)
        return 0

    lax.fori_loop(0, len(WORDS), group, 0)

    for piece in range(2):
        for d in (1, 3, 2):
            y_copy(0, d, piece).wait_recv()
        zh_copy(piece).wait_recv()
        out[:, PART[piece]] = share_sum(0, piece) + zh_in[piece].astype(jnp.float32)

    def sent(k, _):
        core_copy(k).wait_send()
        hc_copy(k).wait_send()
        for way in range(2):
            for copy in (far_copy, near_copy, relay_copy, hx_copy, pass_copy):
                copy(k, way).wait_send()
        for d in (1, 2, 3):
            z_copy(k, d).wait_send()
            hz_copy(k, d).wait_send()
        return 0

    lax.fori_loop(0, CHUNKS, sent, 0)
    for copy in act_sends():
        copy.wait_send()
    for piece in range(2):
        for copy in (*act_forwards(piece), zh_copy(piece)):
            copy.wait_send()
        for half in range(2):
            for d in (1, 2, 3):
                y_copy(half, d, piece).wait_send()


def fused(act, blocks_one, pattern_one, count_one, blocks_two, pattern_two, count_two):
    bf16, f32 = jnp.bfloat16, jnp.float32
    dma = pltpu.SemaphoreType.DMA
    whole = pl.BlockSpec(memory_space=pltpu.VMEM)
    apart = pl.BlockSpec(memory_space=pl.ANY)
    scratch = [
        pltpu.VMEM((2, 1, SLOTS), jnp.int32),
        pltpu.SMEM((2, 1, 1), jnp.int32),
        pltpu.VMEM((SLOTS + 1, BLK, BLK), bf16),
        pltpu.VMEM((SLOTS + 1, BLK, BLK), bf16),
        pltpu.VMEM((NARROW, WIDE), bf16),
        pltpu.VMEM((WIDE, NARROW), bf16),
        pltpu.VMEM((CHUNKS, ROWS, NARROW), bf16),
        pltpu.VMEM((CHUNKS, ROWS, WIDE), f32),
        pltpu.VMEM((CHUNKS, HALF, WIDE), f32),
        pltpu.VMEM((CHUNKS, HALF, WIDE), bf16),
        pltpu.VMEM((CHUNKS, 2, PIECE, WIDE // 2), bf16),
        pltpu.VMEM((CHUNKS, 2, PIECE, WIDE // 2), bf16),
        pltpu.VMEM((CHUNKS, 2, PIECE, WIDE // 2), bf16),
        pltpu.VMEM((CHUNKS, 2, PIECE, WIDE // 2), bf16),
        pltpu.VMEM((CHUNKS, PIECE, WIDE), f32),
        pltpu.VMEM((CHUNKS, PIECE, WIDE), Z_TYPE),
        pltpu.VMEM((CHUNKS, 3, PIECE, NARROW), Z_TYPE),
        pltpu.VMEM((CHUNKS, ROWS, WIDE), bf16),
        pltpu.VMEM((ROWS, NARROW // 2), f32),
        pltpu.VMEM((2, 2, ROWS, NARROW // 2), f32),
        pltpu.VMEM((2, 3, 2, ROWS, NARROW // 2), bf16),
        pltpu.VMEM((2, 3, 2, ROWS, NARROW // 2), bf16),
        pltpu.VMEM((2, ROWS, NARROW // 2), bf16),
        pltpu.VMEM((2, ROWS, NARROW // 2), bf16),
        pltpu.VMEM((2, LANES), jnp.int32),
        pltpu.SMEM((2, LANES), jnp.int32),
        dma((8,)),
    ]
    one, two, three = (CHUNKS,), (CHUNKS, 2), (CHUNKS, 3)
    for shape in (two, one, two, two, two, three, three, two, two, one, (2, 3, 2), (2,)):
        scratch += [dma(shape), dma(shape)]
    return pl.pallas_call(
        kernel,
        name="fused_layers",
        out_shape=jax.ShapeDtypeStruct((ROWS, NARROW), f32),
        in_specs=[apart] * 7,
        out_specs=whole,
        scratch_shapes=scratch,
        compiler_params=pltpu.CompilerParams(collective_id=0, has_side_effects=True, vmem_limit_bytes=56 << 20),
    )(act, blocks_one, pattern_one, count_one, blocks_two, pattern_two, count_two)


def shards(activations, blocks_one, pattern_one, count_one, blocks_two, pattern_two, count_two):
    total = fused(
        activations,
        blocks_one.reshape(SLOTS, BLK, BLK),
        pattern_one.reshape(1, SLOTS),
        count_one,
        blocks_two.reshape(SLOTS, BLK, BLK),
        pattern_two.reshape(1, SLOTS),
        count_two,
    )
    return jnp.maximum(total + BIAS, 0.0).astype(jnp.bfloat16)


def solution(mesh):
    return jax.shard_map(
        shards,
        mesh=mesh,
        in_specs=(
            P("col", "row"),
            P("row", "col", None, None, None),
            P("row", "col", None),
            P("row", "col"),
            P("col", "row", None, None, None),
            P("col", "row", None),
            P("col", "row"),
        ),
        out_specs=P("col", "row"),
        check_vma=False,
    )
```

```python
import jax
import jax.numpy as jnp
from jax import lax
from jax.experimental import pallas as pl
from jax.experimental.pallas import tpu as pltpu
from jax.sharding import PartitionSpec as P

MESH = pl.DeviceIdType.MESH
BIAS = -0.3
BLK = 128
SLOTS = 64
LANES = 128
ROWS = 128
WIDE = 2048
NARROW = 512
CHUNKS = 8
HALF, PIECE = ROWS // 2, ROWS // 8
ORDER = (
    (0, 0), (1, 1), (1, 0), (0, 1), (0, 2), (1, 3), (1, 2), (0, 3),
)
AT = {step: k for k, step in enumerate(ORDER)}
STAGES = (
    "first",
    "sum_core",
    "relay",
    "sum_x",
    "sum_z",
    "spread_x",
    "pass_x",
    "spread_core",
    "second",
    "sum_other",
    "build_two",
    "forward",
)
SCHEDULE = (
    80, 0, 3, 88, 11, 4, 89, 8, 2, 19, 7, 12, 5, 10, 27, 6,
    13, 1, 18, 14, 21, 9, 35, 22, 26, 29, 17, 16, 43, 30, 34, 15,
    20, 25, 38, 51, 42, 37, 23, 33, 28, 46, 45, 31, 41, 54, 36, 50,
    53, 39, 49, 24, 62, 44, 58, 61, 70, 57, 47, 59, 69, 32, 52, 65,
    67, 55, 66, 40, 60, 72, 68, 73, 63, 48, 71, 56, 64,
)
STEP = (1, 3)
PART = (pl.ds(0, NARROW // 2), pl.ds(NARROW // 2, NARROW // 2))
SIDE = (pl.ds(0, WIDE // 2), pl.ds(WIDE // 2, WIDE // 2))
Z_TYPE = jnp.bfloat16


PACK, CODES = 4, 128
IDLE = CODES - 1
WORDS = []
for _start in range(0, len(SCHEDULE), PACK):
    _codes = (SCHEDULE[_start : _start + PACK] + (IDLE,) * PACK)[:PACK]
    WORDS.append(sum(code * CODES**n for n, code in enumerate(_codes)))


def kernel(
    act, blocks_one, pattern_one, count_one, blocks_two, pattern_two, count_two, out,
    patterns, counts,
    stored_one, stored_two, tile_one, tile_two, rows_in, part_one, core_in, x_out, far_in, near_in, relay_out, relay_in, z_sum, z_out, z_in, hidden,
    part_two, kept, y_out, y_in, zh_out, zh_in,
    found, table, load_sem, act_send, act_recv, core_send, core_recv, far_send, far_recv, near_send, near_recv, relay_send, relay_recv, z_send, z_recv,
    hz_send, hz_recv, hx_send, hx_recv, pass_send, pass_recv, hc_send, hc_recv, y_send, y_recv, zh_send, zh_recv,
):
    row, col = lax.axis_index("row"), lax.axis_index("col")
    zl, x, core = row // 8, (row // 2) % 4, row % 2
    zh, y = col // 4, col % 4

    def row_at(zl, x, core):
        return ((zl * 4 + x) * 2 + core, col)

    other_core = row_at(zl, x, 1 - core)
    x_peer = [row_at(zl, (x + d) % 4, core) for d in range(4)]
    z_peer = [row_at((zl + d) % 4, x, core) for d in range(4)]
    y_peer = [(row, zh * 4 + (y + d) % 4) for d in range(4)]
    zh_peer = (row, (1 - zh) * 4 + y)

    def send(src, dst, send_sem, recv_sem, device):
        return pltpu.make_async_remote_copy(
            src_ref=src, dst_ref=dst, send_sem=send_sem, recv_sem=recv_sem,
            device_id=device, device_id_type=MESH,
        )

    def act_copy(src, k, piece, device):
        rows = pl.ds(pl.multiple_of(piece * HALF, HALF), HALF)
        return send(src.at[rows], rows_in.at[k, rows], act_send.at[k, piece], act_recv.at[k, piece], device)

    def core_copy(k):
        src = part_one.at[k, pl.ds(pl.multiple_of((1 - core) * HALF, HALF), HALF)]
        return send(src, core_in.at[k], core_send.at[k], core_recv.at[k], other_core)

    def rows_of(step):
        return pl.ds(pl.multiple_of((x + step) % 4 * PIECE, PIECE), PIECE)

    def far_copy(k, way):
        src = x_out.at[k, rows_of(2), SIDE[way]]
        return send(src, far_in.at[k, way], far_send.at[k, way], far_recv.at[k, way], x_peer[STEP[way]])

    def near_copy(k, way):
        src = x_out.at[k, rows_of(STEP[way]), SIDE[1 - way]]
        return send(src, near_in.at[k, way], near_send.at[k, way], near_recv.at[k, way], x_peer[STEP[way]])

    def relay_copy(k, way):
        src = relay_out.at[k, way]
        return send(src, relay_in.at[k, way], relay_send.at[k, way], relay_recv.at[k, way], x_peer[STEP[way]])

    def z_copy(k, d):
        src = z_out.at[k, :, pl.ds(pl.multiple_of((zl + d) % 4 * NARROW, NARROW), NARROW)]
        return send(src, z_in.at[k, d - 1], z_send.at[k, d - 1], z_recv.at[k, d - 1], z_peer[d])

    mine = pl.ds(pl.multiple_of(core * HALF + x * PIECE, PIECE), PIECE)
    my_half = pl.ds(pl.multiple_of(core * HALF, HALF), HALF)
    my_cols = pl.ds(pl.multiple_of(zl * NARROW, NARROW), NARROW)

    def hz_copy(k, d):
        ref = hidden.at[k, mine, my_cols]
        return send(ref, ref, hz_send.at[k, d - 1], hz_recv.at[k, d - 1], z_peer[d])

    def hx_copy(k, way):
        ref = hidden.at[k, mine]
        return send(ref, ref, hx_send.at[k, way], hx_recv.at[k, way], x_peer[STEP[way]])

    def pass_copy(k, way):
        behind = core * HALF + (x + STEP[1 - way]) % 4 * PIECE
        ref = hidden.at[k, pl.ds(pl.multiple_of(behind, PIECE), PIECE), SIDE[way]]
        return send(ref, ref, pass_send.at[k, way], pass_recv.at[k, way], x_peer[STEP[way]])

    def hc_copy(k):
        ref = hidden.at[k, my_half]
        return send(ref, ref, hc_send.at[k], hc_recv.at[k], other_core)

    def y_copy(half, d, piece):
        at = (half, d - 1, piece)
        return send(y_out.at[at], y_in.at[at], y_send.at[at], y_recv.at[at], (row, zh * 4 + (y + d) % 4))

    def zh_copy(piece):
        return send(zh_out.at[piece], zh_in.at[piece], zh_send.at[piece], zh_recv.at[piece], zh_peer)

    def act_sends():
        for piece in range(2):
            yield act_copy(rows_in.at[AT[0, 0]], AT[1, 0], piece, zh_peer)
        for d in (3, 1, 2):
            for piece in range(2):
                yield act_copy(rows_in.at[AT[0, 0]], AT[0, 4 - d], piece, y_peer[d])

    def act_forwards(piece):
        for d in (3, 1, 2):
            yield act_copy(rows_in.at[AT[1, 0]], AT[1, 4 - d], piece, y_peer[d])

    barrier = pltpu.get_barrier_semaphore()
    partners = [other_core, zh_peer, x_peer[1], x_peer[3], *z_peer[1:], *y_peer[1:]]
    for device in partners:
        pl.semaphore_signal(barrier, inc=1, device_id=device, device_id_type=MESH)

    own = AT[0, 0]
    own_load = pltpu.make_async_copy(act, rows_in.at[own], load_sem.at[3])
    facts = [
        pltpu.make_async_copy(src, dst, load_sem.at[n])
        for n, (src, dst) in enumerate(
            (
                (pattern_one, patterns.at[0]),
                (pattern_two, patterns.at[1]),
                (count_one, counts.at[0]),
                (count_two, counts.at[1]),
            ),
            start=4,
        )
    ]
    loads = [
        pltpu.make_async_copy(ref, stored.at[pl.ds(0, SLOTS)], load_sem.at[layer])
        for layer, (ref, stored) in enumerate(((blocks_one, stored_one), (blocks_two, stored_two)))
    ]
    for load in (own_load, *facts, *loads):
        load.start()
    for stored in (stored_one, stored_two):
        stored[SLOTS] = jnp.zeros((BLK, BLK), jnp.bfloat16)
    for fact in facts:
        fact.wait()

    place = lax.broadcasted_iota(jnp.int32, (LANES, LANES), 0)
    slot = lax.broadcasted_iota(jnp.int32, (LANES, LANES), 1)
    for layer in range(2):
        where = jnp.concatenate([patterns[layer], jnp.zeros((1, LANES - SLOTS), jnp.int32)], axis=1)
        hit = (where == place) & (slot < counts[layer, 0, 0])
        found[pl.ds(layer, 1), :] = jnp.min(jnp.where(hit, slot, SLOTS).T, axis=0, keepdims=True)
    fill = pltpu.make_async_copy(found, table, load_sem.at[2])
    fill.start()
    own_load.wait()

    pl.semaphore_wait(barrier, len(partners))
    for copy in act_sends():
        copy.start()
    fill.wait()

    def build(layer, stored, tile, block_cols):
        def put(p, _):
            r = pl.multiple_of(p // block_cols * BLK, BLK)
            c = pl.multiple_of(p % block_cols * BLK, BLK)
            tile[pl.ds(r, BLK), pl.ds(c, BLK)] = stored[table[layer, p]]
            return 0

        loads[layer].wait()
        lax.fori_loop(0, SLOTS, put, 0)

    build(0, stored_one, tile_one, WIDE // BLK)

    def forward(piece):
        act_copy(rows_in.at[AT[0, 0]], AT[1, 0], piece, zh_peer).wait_recv()
        for copy in act_forwards(piece):
            copy.start()

    def first(k):
        @pl.when((k != AT[0, 0]) & (k != AT[1, 0]))
        def _():
            for piece in range(2):
                act_copy(rows_in.at[AT[0, 0]], k, piece, zh_peer).wait_recv()

        for n in range(WIDE // NARROW):
            cols = pl.ds(n * NARROW, NARROW)
            part_one[k, :, cols] = jnp.dot(rows_in[k], tile_one[:, cols], preferred_element_type=jnp.float32)
        core_copy(k).start()

    def sum_core(k):
        core_copy(k).wait_recv()
        x_out[k] = (part_one[k, my_half] + core_in[k]).astype(jnp.bfloat16)
        for way in range(2):
            far_copy(k, way).start()
        for way in range(2):
            near_copy(k, way).start()

    def own_sum(k, step, cols):
        rows = core * HALF + (x + step) % 4 * PIECE
        return part_one[k, pl.ds(pl.multiple_of(rows, PIECE), PIECE), cols] + core_in[k, rows_of(step), cols]

    def relay(k):
        for way in range(2):
            far_copy(k, way).wait_recv()
            total = own_sum(k, STEP[way], SIDE[way]) + far_in[k, way].astype(jnp.float32)
            relay_out[k, way] = total.astype(jnp.bfloat16)
            relay_copy(k, way).start()

    def sum_x(k):
        for way in range(2):
            near_copy(k, way).wait_recv()
            relay_copy(k, way).wait_recv()
        sides = []
        for way in range(2):
            side = own_sum(k, 0, SIDE[way])
            side += near_in[k, 1 - way].astype(jnp.float32) + relay_in[k, way].astype(jnp.float32)
            sides.append(side)
        total = jnp.concatenate(sides, axis=1)
        z_out[k] = total.astype(z_out.dtype)
        for d in (1, 3, 2):
            z_copy(k, d).start()
        z_sum[k] = total

    def sum_z(k):
        for d in (1, 3, 2):
            z_copy(k, d).wait_recv()
        total = z_sum[k, :, my_cols]
        for d in range(3):
            total += z_in[k, d].astype(jnp.float32)
        hidden[k, mine, my_cols] = jnp.maximum(total + BIAS, 0.0).astype(jnp.bfloat16)
        for d in (1, 3, 2):
            hz_copy(k, d).start()

    def spread_x(k):
        for d in (1, 3, 2):
            hz_copy(k, d).wait_recv()
        for way in range(2):
            hx_copy(k, way).start()

    def pass_x(k):
        for way in range(2):
            hx_copy(k, way).wait_recv()
            pass_copy(k, way).start()

    def spread_core(k):
        for way in range(2):
            pass_copy(k, way).wait_recv()
        hc_copy(k).start()

    def second(k):
        hc_copy(k).wait_recv()
        half, d = jnp.int32(ORDER[0][0]), jnp.int32(ORDER[0][1])
        for other, steps in enumerate(ORDER):
            half = jnp.where(k == other, steps[0], half)
            d = jnp.where(k == other, steps[1], d)
        for piece in range(2):
            part_two[...] = jnp.dot(hidden[k], tile_two[:, PART[piece]], preferred_element_type=jnp.float32)

            @pl.when(d == 0)
            def _():
                kept[half, piece] = part_two[...]

            @pl.when(d != 0)
            def _():
                y_out[half, d - 1, piece] = part_two[...].astype(jnp.bfloat16)
                y_copy(half, d, piece).start()

    def share_sum(half, piece):
        total = kept[half, piece]
        for d in range(3):
            total += y_in[half, d, piece].astype(jnp.float32)
        return total

    def sum_other(piece):
        for d in (1, 3, 2):
            y_copy(1, d, piece).wait_recv()
        zh_out[piece] = share_sum(1, piece).astype(zh_out.dtype)
        zh_copy(piece).start()

    def build_two(k):
        build(1, stored_two, tile_two, NARROW // BLK)

    here = locals()
    stages = [here[name] for name in STAGES]

    def group(n, _):
        word = jnp.int32(WORDS[0])
        for m in range(1, len(WORDS)):
            word = jnp.where(n == m, WORDS[m], word)

        def entry(_, word):
            code = lax.rem(word, CODES)
            for number, stage in enumerate(stages):

                @pl.when(lax.div(code, CHUNKS) == number)
                def _():
                    stage(lax.rem(code, CHUNKS))

            return lax.div(word, CODES)

        lax.fori_loop(0, PACK, entry, word)
        return 0

    lax.fori_loop(0, len(WORDS), group, 0)

    for piece in range(2):
        for d in (1, 3, 2):
            y_copy(0, d, piece).wait_recv()
        zh_copy(piece).wait_recv()
        out[:, PART[piece]] = share_sum(0, piece) + zh_in[piece].astype(jnp.float32)

    def sent(k, _):
        core_copy(k).wait_send()
        hc_copy(k).wait_send()
        for way in range(2):
            for copy in (far_copy, near_copy, relay_copy, hx_copy, pass_copy):
                copy(k, way).wait_send()
        for d in (1, 2, 3):
            z_copy(k, d).wait_send()
            hz_copy(k, d).wait_send()
        return 0

    lax.fori_loop(0, CHUNKS, sent, 0)
    for copy in act_sends():
        copy.wait_send()
    for piece in range(2):
        for copy in (*act_forwards(piece), zh_copy(piece)):
            copy.wait_send()
        for half in range(2):
            for d in (1, 2, 3):
                y_copy(half, d, piece).wait_send()


def fused(act, blocks_one, pattern_one, count_one, blocks_two, pattern_two, count_two):
    bf16, f32 = jnp.bfloat16, jnp.float32
    dma = pltpu.SemaphoreType.DMA
    whole = pl.BlockSpec(memory_space=pltpu.VMEM)
    apart = pl.BlockSpec(memory_space=pl.ANY)
    scratch = [
        pltpu.VMEM((2, 1, SLOTS), jnp.int32),
        pltpu.SMEM((2, 1, 1), jnp.int32),
        pltpu.VMEM((SLOTS + 1, BLK, BLK), bf16),
        pltpu.VMEM((SLOTS + 1, BLK, BLK), bf16),
        pltpu.VMEM((NARROW, WIDE), bf16),
        pltpu.VMEM((WIDE, NARROW), bf16),
        pltpu.VMEM((CHUNKS, ROWS, NARROW), bf16),
        pltpu.VMEM((CHUNKS, ROWS, WIDE), f32),
        pltpu.VMEM((CHUNKS, HALF, WIDE), f32),
        pltpu.VMEM((CHUNKS, HALF, WIDE), bf16),
        pltpu.VMEM((CHUNKS, 2, PIECE, WIDE // 2), bf16),
        pltpu.VMEM((CHUNKS, 2, PIECE, WIDE // 2), bf16),
        pltpu.VMEM((CHUNKS, 2, PIECE, WIDE // 2), bf16),
        pltpu.VMEM((CHUNKS, 2, PIECE, WIDE // 2), bf16),
        pltpu.VMEM((CHUNKS, PIECE, WIDE), f32),
        pltpu.VMEM((CHUNKS, PIECE, WIDE), Z_TYPE),
        pltpu.VMEM((CHUNKS, 3, PIECE, NARROW), Z_TYPE),
        pltpu.VMEM((CHUNKS, ROWS, WIDE), bf16),
        pltpu.VMEM((ROWS, NARROW // 2), f32),
        pltpu.VMEM((2, 2, ROWS, NARROW // 2), f32),
        pltpu.VMEM((2, 3, 2, ROWS, NARROW // 2), bf16),
        pltpu.VMEM((2, 3, 2, ROWS, NARROW // 2), bf16),
        pltpu.VMEM((2, ROWS, NARROW // 2), bf16),
        pltpu.VMEM((2, ROWS, NARROW // 2), bf16),
        pltpu.VMEM((2, LANES), jnp.int32),
        pltpu.SMEM((2, LANES), jnp.int32),
        dma((8,)),
    ]
    one, two, three = (CHUNKS,), (CHUNKS, 2), (CHUNKS, 3)
    for shape in (two, one, two, two, two, three, three, two, two, one, (2, 3, 2), (2,)):
        scratch += [dma(shape), dma(shape)]
    return pl.pallas_call(
        kernel,
        name="fused_layers",
        out_shape=jax.ShapeDtypeStruct((ROWS, NARROW), f32),
        in_specs=[apart] * 7,
        out_specs=whole,
        scratch_shapes=scratch,
        compiler_params=pltpu.CompilerParams(collective_id=0, has_side_effects=True, vmem_limit_bytes=53 << 20),
    )(act, blocks_one, pattern_one, count_one, blocks_two, pattern_two, count_two)


def shards(activations, blocks_one, pattern_one, count_one, blocks_two, pattern_two, count_two):
    total = fused(
        pltpu.with_memory_space_constraint(activations, pltpu.MemorySpace.HBM),
        blocks_one.reshape(SLOTS, BLK, BLK),
        pltpu.with_memory_space_constraint(pattern_one.reshape(1, SLOTS), pltpu.MemorySpace.HBM),
        count_one,
        blocks_two.reshape(SLOTS, BLK, BLK),
        pltpu.with_memory_space_constraint(pattern_two.reshape(1, SLOTS), pltpu.MemorySpace.HBM),
        count_two,
    )
    return jnp.maximum(total + BIAS, 0.0).astype(jnp.bfloat16)


def solution(mesh):
    return jax.shard_map(
        shards,
        mesh=mesh,
        in_specs=(
            P("col", "row"),
            P("row", "col", None, None, None),
            P("row", "col", None),
            P("row", "col"),
            P("col", "row", None, None, None),
            P("col", "row", None),
            P("col", "row"),
        ),
        out_specs=P("col", "row"),
        check_vma=False,
    )
```

```python
import jax
import jax.numpy as jnp
from jax import lax
from jax.experimental import pallas as pl
from jax.experimental.pallas import tpu as pltpu
from jax.sharding import PartitionSpec as P

MESH = pl.DeviceIdType.MESH
BIAS = -0.3
BLK = 128
SLOTS = 64
LANES = 128
ROWS = 128
WIDE = 2048
NARROW = 512
CHUNKS = 8
HALF, PIECE = ROWS // 2, ROWS // 8
ORDER = (
    (1, 3), (1, 2), (0, 0), (0, 1), (0, 2), (0, 3), (1, 1), (1, 0),
)
AT = {step: k for k, step in enumerate(ORDER)}
STAGES = (
    "first",
    "sum_core",
    "relay",
    "sum_x",
    "sum_z",
    "spread_x",
    "pass_x",
    "spread_core",
    "second",
    "sum_other",
    "build_two",
    "forward",
)
SCHEDULE = (
    80, 2, 5, 88, 10, 89, 13, 7, 4, 15, 6, 21, 1, 23, 14, 0,
    29, 9, 31, 8, 3, 17, 37, 22, 39, 16, 12, 25, 11, 30, 18, 47,
    24, 20, 33, 19, 45, 38, 32, 55, 28, 41, 26, 46, 27, 40, 36, 49,
    54, 53, 35, 48, 57, 44, 34, 62, 65, 56, 43, 70, 52, 64, 42, 63,
    51, 61, 60, 71, 72, 68, 59, 73, 50, 69, 67, 58, 66,
)
STEP = (1, 3)
PART = (pl.ds(0, NARROW // 2), pl.ds(NARROW // 2, NARROW // 2))
SIDE = (pl.ds(0, WIDE // 2), pl.ds(WIDE // 2, WIDE // 2))
Z_TYPE = jnp.bfloat16


PACK, CODES = 4, 128
IDLE = CODES - 1
WORDS = []
for _start in range(0, len(SCHEDULE), PACK):
    _codes = (SCHEDULE[_start : _start + PACK] + (IDLE,) * PACK)[:PACK]
    WORDS.append(sum(code * CODES**n for n, code in enumerate(_codes)))


def kernel(
    act, blocks_one, pattern_one, count_one, blocks_two, pattern_two, count_two, out,
    patterns, counts,
    stored_one, stored_two, tile_one, tile_two, rows_in, part_one, core_in, x_out, far_in, near_in, relay_out, relay_in, z_sum, z_out, z_in, hidden,
    part_two, kept, y_out, y_in, zh_out, zh_in,
    found, table, load_sem, act_send, act_recv, core_send, core_recv, far_send, far_recv, near_send, near_recv, relay_send, relay_recv, z_send, z_recv,
    hz_send, hz_recv, hx_send, hx_recv, pass_send, pass_recv, hc_send, hc_recv, y_send, y_recv, zh_send, zh_recv,
):
    row, col = lax.axis_index("row"), lax.axis_index("col")
    zl, x, core = row // 8, (row // 2) % 4, row % 2
    zh, y = col // 4, col % 4

    def row_at(zl, x, core):
        return ((zl * 4 + x) * 2 + core, col)

    other_core = row_at(zl, x, 1 - core)
    x_peer = [row_at(zl, (x + d) % 4, core) for d in range(4)]
    z_peer = [row_at((zl + d) % 4, x, core) for d in range(4)]
    y_peer = [(row, zh * 4 + (y + d) % 4) for d in range(4)]
    zh_peer = (row, (1 - zh) * 4 + y)

    def send(src, dst, send_sem, recv_sem, device):
        return pltpu.make_async_remote_copy(
            src_ref=src, dst_ref=dst, send_sem=send_sem, recv_sem=recv_sem,
            device_id=device, device_id_type=MESH,
        )

    def act_copy(src, k, piece, device):
        rows = pl.ds(pl.multiple_of(piece * HALF, HALF), HALF)
        return send(src.at[rows], rows_in.at[k, rows], act_send.at[k, piece], act_recv.at[k, piece], device)

    def core_copy(k):
        src = part_one.at[k, pl.ds(pl.multiple_of((1 - core) * HALF, HALF), HALF)]
        return send(src, core_in.at[k], core_send.at[k], core_recv.at[k], other_core)

    def rows_of(step):
        return pl.ds(pl.multiple_of((x + step) % 4 * PIECE, PIECE), PIECE)

    def far_copy(k, way):
        src = x_out.at[k, rows_of(2), SIDE[way]]
        return send(src, far_in.at[k, way], far_send.at[k, way], far_recv.at[k, way], x_peer[STEP[way]])

    def near_copy(k, way):
        src = x_out.at[k, rows_of(STEP[way]), SIDE[1 - way]]
        return send(src, near_in.at[k, way], near_send.at[k, way], near_recv.at[k, way], x_peer[STEP[way]])

    def relay_copy(k, way):
        src = relay_out.at[k, way]
        return send(src, relay_in.at[k, way], relay_send.at[k, way], relay_recv.at[k, way], x_peer[STEP[way]])

    def z_copy(k, d):
        src = z_out.at[k, :, pl.ds(pl.multiple_of((zl + d) % 4 * NARROW, NARROW), NARROW)]
        return send(src, z_in.at[k, d - 1], z_send.at[k, d - 1], z_recv.at[k, d - 1], z_peer[d])

    mine = pl.ds(pl.multiple_of(core * HALF + x * PIECE, PIECE), PIECE)
    my_half = pl.ds(pl.multiple_of(core * HALF, HALF), HALF)
    my_cols = pl.ds(pl.multiple_of(zl * NARROW, NARROW), NARROW)

    def hz_copy(k, d):
        ref = hidden.at[k, mine, my_cols]
        return send(ref, ref, hz_send.at[k, d - 1], hz_recv.at[k, d - 1], z_peer[d])

    def hx_copy(k, way):
        ref = hidden.at[k, mine]
        return send(ref, ref, hx_send.at[k, way], hx_recv.at[k, way], x_peer[STEP[way]])

    def pass_copy(k, way):
        behind = core * HALF + (x + STEP[1 - way]) % 4 * PIECE
        ref = hidden.at[k, pl.ds(pl.multiple_of(behind, PIECE), PIECE), SIDE[way]]
        return send(ref, ref, pass_send.at[k, way], pass_recv.at[k, way], x_peer[STEP[way]])

    def hc_copy(k):
        ref = hidden.at[k, my_half]
        return send(ref, ref, hc_send.at[k], hc_recv.at[k], other_core)

    def y_copy(half, d, piece):
        at = (half, d - 1, piece)
        return send(y_out.at[at], y_in.at[at], y_send.at[at], y_recv.at[at], (row, zh * 4 + (y + d) % 4))

    def zh_copy(piece):
        return send(zh_out.at[piece], zh_in.at[piece], zh_send.at[piece], zh_recv.at[piece], zh_peer)

    def act_sends():
        for piece in range(2):
            yield act_copy(rows_in.at[AT[0, 0]], AT[1, 0], piece, zh_peer)
        for d in (3, 1, 2):
            for piece in range(2):
                yield act_copy(rows_in.at[AT[0, 0]], AT[0, 4 - d], piece, y_peer[d])

    def act_forwards(piece):
        for d in (3, 1, 2):
            yield act_copy(rows_in.at[AT[1, 0]], AT[1, 4 - d], piece, y_peer[d])

    barrier = pltpu.get_barrier_semaphore()
    partners = [other_core, zh_peer, x_peer[1], x_peer[3], *z_peer[1:], *y_peer[1:]]
    for device in partners:
        pl.semaphore_signal(barrier, inc=1, device_id=device, device_id_type=MESH)

    own = AT[0, 0]
    own_load = pltpu.make_async_copy(act, rows_in.at[own], load_sem.at[3])
    facts = [
        pltpu.make_async_copy(src, dst, load_sem.at[n])
        for n, (src, dst) in enumerate(
            (
                (pattern_one, patterns.at[0]),
                (pattern_two, patterns.at[1]),
                (count_one, counts.at[0]),
                (count_two, counts.at[1]),
            ),
            start=4,
        )
    ]
    loads = [
        pltpu.make_async_copy(ref, stored.at[pl.ds(0, SLOTS)], load_sem.at[layer])
        for layer, (ref, stored) in enumerate(((blocks_one, stored_one), (blocks_two, stored_two)))
    ]
    for load in (own_load, *facts, *loads):
        load.start()
    for stored in (stored_one, stored_two):
        stored[SLOTS] = jnp.zeros((BLK, BLK), jnp.bfloat16)
    for fact in facts:
        fact.wait()

    place = lax.broadcasted_iota(jnp.int32, (LANES, LANES), 0)
    slot = lax.broadcasted_iota(jnp.int32, (LANES, LANES), 1)
    for layer in range(2):
        where = jnp.concatenate([patterns[layer], jnp.zeros((1, LANES - SLOTS), jnp.int32)], axis=1)
        hit = (where == place) & (slot < counts[layer, 0, 0])
        found[pl.ds(layer, 1), :] = jnp.min(jnp.where(hit, slot, SLOTS).T, axis=0, keepdims=True)
    fill = pltpu.make_async_copy(found, table, load_sem.at[2])
    fill.start()
    own_load.wait()

    pl.semaphore_wait(barrier, len(partners))
    for copy in act_sends():
        copy.start()
    fill.wait()

    def build(layer, stored, tile, block_cols):
        def put(p, _):
            r = pl.multiple_of(p // block_cols * BLK, BLK)
            c = pl.multiple_of(p % block_cols * BLK, BLK)
            tile[pl.ds(r, BLK), pl.ds(c, BLK)] = stored[table[layer, p]]
            return 0

        loads[layer].wait()
        lax.fori_loop(0, SLOTS, put, 0)

    build(0, stored_one, tile_one, WIDE // BLK)

    def forward(piece):
        act_copy(rows_in.at[AT[0, 0]], AT[1, 0], piece, zh_peer).wait_recv()
        for copy in act_forwards(piece):
            copy.start()

    def first(k):
        @pl.when((k != AT[0, 0]) & (k != AT[1, 0]))
        def _():
            for piece in range(2):
                act_copy(rows_in.at[AT[0, 0]], k, piece, zh_peer).wait_recv()

        for n in range(WIDE // NARROW):
            cols = pl.ds(n * NARROW, NARROW)
            part_one[k, :, cols] = jnp.dot(rows_in[k], tile_one[:, cols], preferred_element_type=jnp.float32)
        core_copy(k).start()

    def sum_core(k):
        core_copy(k).wait_recv()
        x_out[k] = (part_one[k, my_half] + core_in[k]).astype(jnp.bfloat16)
        for way in range(2):
            far_copy(k, way).start()
        for way in range(2):
            near_copy(k, way).start()

    def own_sum(k, step, cols):
        rows = core * HALF + (x + step) % 4 * PIECE
        return part_one[k, pl.ds(pl.multiple_of(rows, PIECE), PIECE), cols] + core_in[k, rows_of(step), cols]

    def relay(k):
        for way in range(2):
            far_copy(k, way).wait_recv()
            total = own_sum(k, STEP[way], SIDE[way]) + far_in[k, way].astype(jnp.float32)
            relay_out[k, way] = total.astype(jnp.bfloat16)
            relay_copy(k, way).start()

    def sum_x(k):
        for way in range(2):
            near_copy(k, way).wait_recv()
            relay_copy(k, way).wait_recv()
        sides = []
        for way in range(2):
            side = own_sum(k, 0, SIDE[way])
            side += near_in[k, 1 - way].astype(jnp.float32) + relay_in[k, way].astype(jnp.float32)
            sides.append(side)
        total = jnp.concatenate(sides, axis=1)
        z_out[k] = total.astype(z_out.dtype)
        for d in (1, 3, 2):
            z_copy(k, d).start()
        z_sum[k] = total

    def sum_z(k):
        for d in (1, 3, 2):
            z_copy(k, d).wait_recv()
        total = z_sum[k, :, my_cols]
        for d in range(3):
            total += z_in[k, d].astype(jnp.float32)
        hidden[k, mine, my_cols] = jnp.maximum(total + BIAS, 0.0).astype(jnp.bfloat16)
        for d in (1, 3, 2):
            hz_copy(k, d).start()

    def spread_x(k):
        for d in (1, 3, 2):
            hz_copy(k, d).wait_recv()
        for way in range(2):
            hx_copy(k, way).start()

    def pass_x(k):
        for way in range(2):
            hx_copy(k, way).wait_recv()
            pass_copy(k, way).start()

    def spread_core(k):
        for way in range(2):
            pass_copy(k, way).wait_recv()
        hc_copy(k).start()

    def second(k):
        hc_copy(k).wait_recv()
        half, d = jnp.int32(ORDER[0][0]), jnp.int32(ORDER[0][1])
        for other, steps in enumerate(ORDER):
            half = jnp.where(k == other, steps[0], half)
            d = jnp.where(k == other, steps[1], d)
        for piece in range(2):
            part_two[...] = jnp.dot(hidden[k], tile_two[:, PART[piece]], preferred_element_type=jnp.float32)

            @pl.when(d == 0)
            def _():
                kept[half, piece] = part_two[...]

            @pl.when(d != 0)
            def _():
                y_out[half, d - 1, piece] = part_two[...].astype(jnp.bfloat16)
                y_copy(half, d, piece).start()

    def share_sum(half, piece):
        total = kept[half, piece]
        for d in range(3):
            total += y_in[half, d, piece].astype(jnp.float32)
        return total

    def sum_other(piece):
        for d in (1, 3, 2):
            y_copy(1, d, piece).wait_recv()
        zh_out[piece] = share_sum(1, piece).astype(zh_out.dtype)
        zh_copy(piece).start()

    def build_two(k):
        build(1, stored_two, tile_two, NARROW // BLK)

    here = locals()
    stages = [here[name] for name in STAGES]

    def group(n, _):
        word = jnp.int32(WORDS[0])
        for m in range(1, len(WORDS)):
            word = jnp.where(n == m, WORDS[m], word)

        def entry(_, word):
            code = lax.rem(word, CODES)
            number, k = lax.div(code, CHUNKS), lax.rem(code, CHUNKS)

            def choose(low, high):
                if high - low == 1:
                    stages[low](k)
                    return
                middle = (low + high) // 2
                pl.when(number < middle)(lambda: choose(low, middle))
                pl.when(number >= middle)(lambda: choose(middle, high))

            pl.when(number < len(stages))(lambda: choose(0, len(stages)))
            return lax.div(word, CODES)

        lax.fori_loop(0, PACK, entry, word)
        return 0

    lax.fori_loop(0, len(WORDS), group, 0)

    for piece in range(2):
        for d in (1, 3, 2):
            y_copy(0, d, piece).wait_recv()
        zh_copy(piece).wait_recv()
        out[:, PART[piece]] = share_sum(0, piece) + zh_in[piece].astype(jnp.float32)

    def sent(k, _):
        core_copy(k).wait_send()
        hc_copy(k).wait_send()
        for way in range(2):
            for copy in (far_copy, near_copy, relay_copy, hx_copy, pass_copy):
                copy(k, way).wait_send()
        for d in (1, 2, 3):
            z_copy(k, d).wait_send()
            hz_copy(k, d).wait_send()
        return 0

    lax.fori_loop(0, CHUNKS, sent, 0)
    for copy in act_sends():
        copy.wait_send()
    for piece in range(2):
        for copy in (*act_forwards(piece), zh_copy(piece)):
            copy.wait_send()
        for half in range(2):
            for d in (1, 2, 3):
                y_copy(half, d, piece).wait_send()


def fused(act, blocks_one, pattern_one, count_one, blocks_two, pattern_two, count_two):
    bf16, f32 = jnp.bfloat16, jnp.float32
    dma = pltpu.SemaphoreType.DMA
    whole = pl.BlockSpec(memory_space=pltpu.VMEM)
    apart = pl.BlockSpec(memory_space=pl.ANY)
    scratch = [
        pltpu.VMEM((2, 1, SLOTS), jnp.int32),
        pltpu.SMEM((2, 1, 1), jnp.int32),
        pltpu.VMEM((SLOTS + 1, BLK, BLK), bf16),
        pltpu.VMEM((SLOTS + 1, BLK, BLK), bf16),
        pltpu.VMEM((NARROW, WIDE), bf16),
        pltpu.VMEM((WIDE, NARROW), bf16),
        pltpu.VMEM((CHUNKS, ROWS, NARROW), bf16),
        pltpu.VMEM((CHUNKS, ROWS, WIDE), f32),
        pltpu.VMEM((CHUNKS, HALF, WIDE), f32),
        pltpu.VMEM((CHUNKS, HALF, WIDE), bf16),
        pltpu.VMEM((CHUNKS, 2, PIECE, WIDE // 2), bf16),
        pltpu.VMEM((CHUNKS, 2, PIECE, WIDE // 2), bf16),
        pltpu.VMEM((CHUNKS, 2, PIECE, WIDE // 2), bf16),
        pltpu.VMEM((CHUNKS, 2, PIECE, WIDE // 2), bf16),
        pltpu.VMEM((CHUNKS, PIECE, WIDE), f32),
        pltpu.VMEM((CHUNKS, PIECE, WIDE), Z_TYPE),
        pltpu.VMEM((CHUNKS, 3, PIECE, NARROW), Z_TYPE),
        pltpu.VMEM((CHUNKS, ROWS, WIDE), bf16),
        pltpu.VMEM((ROWS, NARROW // 2), f32),
        pltpu.VMEM((2, 2, ROWS, NARROW // 2), f32),
        pltpu.VMEM((2, 3, 2, ROWS, NARROW // 2), bf16),
        pltpu.VMEM((2, 3, 2, ROWS, NARROW // 2), bf16),
        pltpu.VMEM((2, ROWS, NARROW // 2), bf16),
        pltpu.VMEM((2, ROWS, NARROW // 2), bf16),
        pltpu.VMEM((2, LANES), jnp.int32),
        pltpu.SMEM((2, LANES), jnp.int32),
        dma((8,)),
    ]
    one, two, three = (CHUNKS,), (CHUNKS, 2), (CHUNKS, 3)
    for shape in (two, one, two, two, two, three, three, two, two, one, (2, 3, 2), (2,)):
        scratch += [dma(shape), dma(shape)]
    return pl.pallas_call(
        kernel,
        name="fused_layers",
        out_shape=jax.ShapeDtypeStruct((ROWS, NARROW), f32),
        in_specs=[apart] * 7,
        out_specs=whole,
        scratch_shapes=scratch,
        compiler_params=pltpu.CompilerParams(collective_id=0, has_side_effects=True, vmem_limit_bytes=53 << 20),
    )(act, blocks_one, pattern_one, count_one, blocks_two, pattern_two, count_two)


def shards(activations, blocks_one, pattern_one, count_one, blocks_two, pattern_two, count_two):
    total = fused(
        pltpu.with_memory_space_constraint(activations, pltpu.MemorySpace.HBM),
        blocks_one.reshape(SLOTS, BLK, BLK),
        pltpu.with_memory_space_constraint(pattern_one.reshape(1, SLOTS), pltpu.MemorySpace.HBM),
        count_one,
        blocks_two.reshape(SLOTS, BLK, BLK),
        pltpu.with_memory_space_constraint(pattern_two.reshape(1, SLOTS), pltpu.MemorySpace.HBM),
        count_two,
    )
    return jnp.maximum(total + BIAS, 0.0).astype(jnp.bfloat16)


def solution(mesh):
    return jax.shard_map(
        shards,
        mesh=mesh,
        in_specs=(
            P("col", "row"),
            P("row", "col", None, None, None),
            P("row", "col", None),
            P("row", "col"),
            P("col", "row", None, None, None),
            P("col", "row", None),
            P("col", "row"),
        ),
        out_specs=P("col", "row"),
        check_vma=False,
    )
```

```python
import jax
import jax.numpy as jnp
from jax import lax
from jax.experimental import pallas as pl
from jax.experimental.pallas import tpu as pltpu
from jax.sharding import PartitionSpec as P

MESH = pl.DeviceIdType.MESH
BIAS = -0.3
BLK = 128
SLOTS = 64
LANES = 128
ROWS = 128
WIDE = 2048
NARROW = 512
CHUNKS = 8
HALF, PIECE = ROWS // 2, ROWS // 8
ORDER = (
    (1, 3), (1, 2), (0, 0), (0, 1), (0, 2), (0, 3), (1, 1), (1, 0),
)
AT = {step: k for k, step in enumerate(ORDER)}
STAGES = (
    "first",
    "sum_core",
    "relay",
    "sum_x",
    "sum_z",
    "spread_x",
    "pass_x",
    "spread_core",
    "second",
    "sum_other",
    "build_two",
    "forward",
)
SCHEDULE = (
    80, 2, 5, 88, 10, 89, 13, 7, 4, 15, 6, 21, 1, 23, 14, 0,
    29, 9, 31, 8, 3, 17, 37, 22, 39, 16, 12, 25, 11, 30, 18, 47,
    24, 20, 33, 19, 45, 38, 32, 55, 28, 41, 26, 46, 27, 40, 36, 49,
    54, 53, 35, 48, 57, 44, 34, 62, 65, 56, 43, 70, 52, 64, 42, 63,
    51, 61, 60, 71, 72, 68, 59, 73, 50, 69, 67, 58, 66,
)
STEP = (1, 3)
PART = (pl.ds(0, NARROW // 2), pl.ds(NARROW // 2, NARROW // 2))
SIDE = (pl.ds(0, WIDE // 2), pl.ds(WIDE // 2, WIDE // 2))
Z_TYPE = jnp.bfloat16


PACK, CODES = 4, 128
IDLE = CODES - 1
WORDS = []
for _start in range(0, len(SCHEDULE), PACK):
    _codes = (SCHEDULE[_start : _start + PACK] + (IDLE,) * PACK)[:PACK]
    WORDS.append(sum(code * CODES**n for n, code in enumerate(_codes)))


def kernel(
    act, blocks_one, pattern_one, count_one, blocks_two, pattern_two, count_two, out,
    patterns, counts,
    stored_one, stored_two, tile_one, tile_two, rows_in, part_one, core_in, x_out, far_in, near_in, relay_out, relay_in, z_sum, z_out, z_in, hidden,
    part_two, kept, y_out, y_in, zh_out, zh_in,
    found, table, load_sem, act_send, act_recv, core_send, core_recv, far_send, far_recv, near_send, near_recv, relay_send, relay_recv, z_send, z_recv,
    hz_send, hz_recv, hx_send, hx_recv, pass_send, pass_recv, hc_send, hc_recv, y_send, y_recv, zh_send, zh_recv,
):
    row, col = lax.axis_index("row"), lax.axis_index("col")
    zl, x, core = row // 8, (row // 2) % 4, row % 2
    zh, y = col // 4, col % 4

    def row_at(zl, x, core):
        return ((zl * 4 + x) * 2 + core, col)

    other_core = row_at(zl, x, 1 - core)
    x_peer = [row_at(zl, (x + d) % 4, core) for d in range(4)]
    z_peer = [row_at((zl + d) % 4, x, core) for d in range(4)]
    y_peer = [(row, zh * 4 + (y + d) % 4) for d in range(4)]
    zh_peer = (row, (1 - zh) * 4 + y)

    def send(src, dst, send_sem, recv_sem, device):
        return pltpu.make_async_remote_copy(
            src_ref=src, dst_ref=dst, send_sem=send_sem, recv_sem=recv_sem,
            device_id=device, device_id_type=MESH,
        )

    def act_copy(src, k, piece, device):
        rows = pl.ds(pl.multiple_of(piece * HALF, HALF), HALF)
        return send(src.at[rows], rows_in.at[k, rows], act_send.at[k, piece], act_recv.at[k, piece], device)

    def core_copy(k):
        src = part_one.at[k, pl.ds(pl.multiple_of((1 - core) * HALF, HALF), HALF)]
        return send(src, core_in.at[k], core_send.at[k], core_recv.at[k], other_core)

    def rows_of(step):
        return pl.ds(pl.multiple_of((x + step) % 4 * PIECE, PIECE), PIECE)

    def far_copy(k, way):
        src = x_out.at[k, rows_of(2), SIDE[way]]
        return send(src, far_in.at[k, way], far_send.at[k, way], far_recv.at[k, way], x_peer[STEP[way]])

    def near_copy(k, way):
        src = x_out.at[k, rows_of(STEP[way]), SIDE[1 - way]]
        return send(src, near_in.at[k, way], near_send.at[k, way], near_recv.at[k, way], x_peer[STEP[way]])

    def relay_copy(k, way):
        src = relay_out.at[k, way]
        return send(src, relay_in.at[k, way], relay_send.at[k, way], relay_recv.at[k, way], x_peer[STEP[way]])

    def z_copy(k, d):
        src = z_out.at[k, :, pl.ds(pl.multiple_of((zl + d) % 4 * NARROW, NARROW), NARROW)]
        return send(src, z_in.at[k, d - 1], z_send.at[k, d - 1], z_recv.at[k, d - 1], z_peer[d])

    mine = pl.ds(pl.multiple_of(core * HALF + x * PIECE, PIECE), PIECE)
    my_half = pl.ds(pl.multiple_of(core * HALF, HALF), HALF)
    my_cols = pl.ds(pl.multiple_of(zl * NARROW, NARROW), NARROW)

    def hz_copy(k, d):
        ref = hidden.at[k, mine, my_cols]
        return send(ref, ref, hz_send.at[k, d - 1], hz_recv.at[k, d - 1], z_peer[d])

    def hx_copy(k, way):
        ref = hidden.at[k, mine]
        return send(ref, ref, hx_send.at[k, way], hx_recv.at[k, way], x_peer[STEP[way]])

    def pass_copy(k, way):
        behind = core * HALF + (x + STEP[1 - way]) % 4 * PIECE
        ref = hidden.at[k, pl.ds(pl.multiple_of(behind, PIECE), PIECE), SIDE[way]]
        return send(ref, ref, pass_send.at[k, way], pass_recv.at[k, way], x_peer[STEP[way]])

    def hc_copy(k):
        ref = hidden.at[k, my_half]
        return send(ref, ref, hc_send.at[k], hc_recv.at[k], other_core)

    def y_copy(half, d, piece):
        at = (half, d - 1, piece)
        return send(y_out.at[at], y_in.at[at], y_send.at[at], y_recv.at[at], (row, zh * 4 + (y + d) % 4))

    def zh_copy(piece):
        return send(zh_out.at[piece], zh_in.at[piece], zh_send.at[piece], zh_recv.at[piece], zh_peer)

    def act_sends():
        for piece in range(2):
            yield act_copy(rows_in.at[AT[0, 0]], AT[1, 0], piece, zh_peer)
        for d in (3, 1, 2):
            for piece in range(2):
                yield act_copy(rows_in.at[AT[0, 0]], AT[0, 4 - d], piece, y_peer[d])

    def act_forwards(piece):
        for d in (3, 1, 2):
            yield act_copy(rows_in.at[AT[1, 0]], AT[1, 4 - d], piece, y_peer[d])

    barrier = pltpu.get_barrier_semaphore()
    partners = [other_core, zh_peer, x_peer[1], x_peer[3], *z_peer[1:], *y_peer[1:]]
    for device in partners:
        pl.semaphore_signal(barrier, inc=1, device_id=device, device_id_type=MESH)

    own = AT[0, 0]
    own_load = pltpu.make_async_copy(act, rows_in.at[own], load_sem.at[3])
    facts = [
        pltpu.make_async_copy(src, dst, load_sem.at[n])
        for n, (src, dst) in enumerate(
            (
                (pattern_one, patterns.at[0]),
                (pattern_two, patterns.at[1]),
                (count_one, counts.at[0]),
                (count_two, counts.at[1]),
            ),
            start=4,
        )
    ]
    loads = [
        pltpu.make_async_copy(ref, stored.at[pl.ds(0, SLOTS)], load_sem.at[layer])
        for layer, (ref, stored) in enumerate(((blocks_one, stored_one), (blocks_two, stored_two)))
    ]
    for load in (own_load, *facts, loads[0]):
        load.start()
    for stored in (stored_one, stored_two):
        stored[SLOTS] = jnp.zeros((BLK, BLK), jnp.bfloat16)
    for fact in facts:
        fact.wait()

    place = lax.broadcasted_iota(jnp.int32, (LANES, LANES), 0)
    slot = lax.broadcasted_iota(jnp.int32, (LANES, LANES), 1)
    for layer in range(2):
        where = jnp.concatenate([patterns[layer], jnp.zeros((1, LANES - SLOTS), jnp.int32)], axis=1)
        hit = (where == place) & (slot < counts[layer, 0, 0])
        found[pl.ds(layer, 1), :] = jnp.min(jnp.where(hit, slot, SLOTS).T, axis=0, keepdims=True)
    fill = pltpu.make_async_copy(found, table, load_sem.at[2])
    fill.start()
    own_load.wait()

    pl.semaphore_wait(barrier, len(partners))
    for copy in act_sends():
        copy.start()
    fill.wait()

    def build(layer, stored, tile, block_cols):
        def put(p, _):
            r = pl.multiple_of(p // block_cols * BLK, BLK)
            c = pl.multiple_of(p % block_cols * BLK, BLK)
            tile[pl.ds(r, BLK), pl.ds(c, BLK)] = stored[table[layer, p]]
            return 0

        loads[layer].wait()
        lax.fori_loop(0, SLOTS, put, 0)

    build(0, stored_one, tile_one, WIDE // BLK)
    loads[1].start()

    def forward(piece):
        act_copy(rows_in.at[AT[0, 0]], AT[1, 0], piece, zh_peer).wait_recv()
        for copy in act_forwards(piece):
            copy.start()

    def first(k):
        @pl.when((k != AT[0, 0]) & (k != AT[1, 0]))
        def _():
            for piece in range(2):
                act_copy(rows_in.at[AT[0, 0]], k, piece, zh_peer).wait_recv()

        for n in range(WIDE // NARROW):
            cols = pl.ds(n * NARROW, NARROW)
            part_one[k, :, cols] = jnp.dot(rows_in[k], tile_one[:, cols], preferred_element_type=jnp.float32)
        core_copy(k).start()

    def sum_core(k):
        core_copy(k).wait_recv()
        x_out[k] = (part_one[k, my_half] + core_in[k]).astype(jnp.bfloat16)
        for way in range(2):
            far_copy(k, way).start()
        for way in range(2):
            near_copy(k, way).start()

    def own_sum(k, step, cols):
        rows = core * HALF + (x + step) % 4 * PIECE
        return part_one[k, pl.ds(pl.multiple_of(rows, PIECE), PIECE), cols] + core_in[k, rows_of(step), cols]

    def relay(k):
        for way in range(2):
            far_copy(k, way).wait_recv()
            total = own_sum(k, STEP[way], SIDE[way]) + far_in[k, way].astype(jnp.float32)
            relay_out[k, way] = total.astype(jnp.bfloat16)
            relay_copy(k, way).start()

    def sum_x(k):
        for way in range(2):
            near_copy(k, way).wait_recv()
            relay_copy(k, way).wait_recv()
        sides = []
        for way in range(2):
            side = own_sum(k, 0, SIDE[way])
            side += near_in[k, 1 - way].astype(jnp.float32) + relay_in[k, way].astype(jnp.float32)
            sides.append(side)
        total = jnp.concatenate(sides, axis=1)
        z_out[k] = total.astype(z_out.dtype)
        for d in (1, 3, 2):
            z_copy(k, d).start()
        z_sum[k] = total

    def sum_z(k):
        for d in (1, 3, 2):
            z_copy(k, d).wait_recv()
        total = z_sum[k, :, my_cols]
        for d in range(3):
            total += z_in[k, d].astype(jnp.float32)
        hidden[k, mine, my_cols] = jnp.maximum(total + BIAS, 0.0).astype(jnp.bfloat16)
        for d in (1, 3, 2):
            hz_copy(k, d).start()

    def spread_x(k):
        for d in (1, 3, 2):
            hz_copy(k, d).wait_recv()
        for way in range(2):
            hx_copy(k, way).start()

    def pass_x(k):
        for way in range(2):
            hx_copy(k, way).wait_recv()
            pass_copy(k, way).start()

    def spread_core(k):
        for way in range(2):
            pass_copy(k, way).wait_recv()
        hc_copy(k).start()

    def second(k):
        hc_copy(k).wait_recv()
        half, d = jnp.int32(ORDER[0][0]), jnp.int32(ORDER[0][1])
        for other, steps in enumerate(ORDER):
            half = jnp.where(k == other, steps[0], half)
            d = jnp.where(k == other, steps[1], d)
        for piece in range(2):
            part_two[...] = jnp.dot(hidden[k], tile_two[:, PART[piece]], preferred_element_type=jnp.float32)

            @pl.when(d == 0)
            def _():
                kept[half, piece] = part_two[...]

            @pl.when(d != 0)
            def _():
                y_out[half, d - 1, piece] = part_two[...].astype(jnp.bfloat16)
                y_copy(half, d, piece).start()

    def share_sum(half, piece):
        total = kept[half, piece]
        for d in range(3):
            total += y_in[half, d, piece].astype(jnp.float32)
        return total

    def sum_other(piece):
        for d in (1, 3, 2):
            y_copy(1, d, piece).wait_recv()
        zh_out[piece] = share_sum(1, piece).astype(zh_out.dtype)
        zh_copy(piece).start()

    def build_two(k):
        build(1, stored_two, tile_two, NARROW // BLK)

    here = locals()
    stages = [here[name] for name in STAGES]

    def group(n, _):
        word = jnp.int32(WORDS[0])
        for m in range(1, len(WORDS)):
            word = jnp.where(n == m, WORDS[m], word)

        def entry(_, word):
            code = lax.rem(word, CODES)
            number, k = lax.div(code, CHUNKS), lax.rem(code, CHUNKS)

            def choose(low, high):
                if high - low == 1:
                    stages[low](k)
                    return
                middle = (low + high) // 2
                pl.when(number < middle)(lambda: choose(low, middle))
                pl.when(number >= middle)(lambda: choose(middle, high))

            pl.when(number < len(stages))(lambda: choose(0, len(stages)))
            return lax.div(word, CODES)

        lax.fori_loop(0, PACK, entry, word)
        return 0

    lax.fori_loop(0, len(WORDS), group, 0)

    def sent(k, _):
        core_copy(k).wait_send()
        hc_copy(k).wait_send()
        for way in range(2):
            for copy in (far_copy, near_copy, relay_copy, hx_copy, pass_copy):
                copy(k, way).wait_send()
        for d in (1, 2, 3):
            z_copy(k, d).wait_send()
            hz_copy(k, d).wait_send()
        return 0

    lax.fori_loop(0, CHUNKS, sent, 0)
    for copy in act_sends():
        copy.wait_send()
    for piece in range(2):
        for copy in act_forwards(piece):
            copy.wait_send()
        for half in range(2):
            for d in (1, 2, 3):
                y_copy(half, d, piece).wait_send()

    for piece in range(2):
        for d in (1, 3, 2):
            y_copy(0, d, piece).wait_recv()
        zh_copy(piece).wait_recv()
        out[:, PART[piece]] = share_sum(0, piece) + zh_in[piece].astype(jnp.float32)
        zh_copy(piece).wait_send()


def fused(act, blocks_one, pattern_one, count_one, blocks_two, pattern_two, count_two):
    bf16, f32 = jnp.bfloat16, jnp.float32
    dma = pltpu.SemaphoreType.DMA
    whole = pl.BlockSpec(memory_space=pltpu.VMEM)
    apart = pl.BlockSpec(memory_space=pl.ANY)
    scratch = [
        pltpu.VMEM((2, 1, SLOTS), jnp.int32),
        pltpu.SMEM((2, 1, 1), jnp.int32),
        pltpu.VMEM((SLOTS + 1, BLK, BLK), bf16),
        pltpu.VMEM((SLOTS + 1, BLK, BLK), bf16),
        pltpu.VMEM((NARROW, WIDE), bf16),
        pltpu.VMEM((WIDE, NARROW), bf16),
        pltpu.VMEM((CHUNKS, ROWS, NARROW), bf16),
        pltpu.VMEM((CHUNKS, ROWS, WIDE), f32),
        pltpu.VMEM((CHUNKS, HALF, WIDE), f32),
        pltpu.VMEM((CHUNKS, HALF, WIDE), bf16),
        pltpu.VMEM((CHUNKS, 2, PIECE, WIDE // 2), bf16),
        pltpu.VMEM((CHUNKS, 2, PIECE, WIDE // 2), bf16),
        pltpu.VMEM((CHUNKS, 2, PIECE, WIDE // 2), bf16),
        pltpu.VMEM((CHUNKS, 2, PIECE, WIDE // 2), bf16),
        pltpu.VMEM((CHUNKS, PIECE, WIDE), f32),
        pltpu.VMEM((CHUNKS, PIECE, WIDE), Z_TYPE),
        pltpu.VMEM((CHUNKS, 3, PIECE, NARROW), Z_TYPE),
        pltpu.VMEM((CHUNKS, ROWS, WIDE), bf16),
        pltpu.VMEM((ROWS, NARROW // 2), f32),
        pltpu.VMEM((2, 2, ROWS, NARROW // 2), f32),
        pltpu.VMEM((2, 3, 2, ROWS, NARROW // 2), bf16),
        pltpu.VMEM((2, 3, 2, ROWS, NARROW // 2), bf16),
        pltpu.VMEM((2, ROWS, NARROW // 2), bf16),
        pltpu.VMEM((2, ROWS, NARROW // 2), bf16),
        pltpu.VMEM((2, LANES), jnp.int32),
        pltpu.SMEM((2, LANES), jnp.int32),
        dma((8,)),
    ]
    one, two, three = (CHUNKS,), (CHUNKS, 2), (CHUNKS, 3)
    for shape in (two, one, two, two, two, three, three, two, two, one, (2, 3, 2), (2,)):
        scratch += [dma(shape), dma(shape)]
    return pl.pallas_call(
        kernel,
        name="fused_layers",
        out_shape=jax.ShapeDtypeStruct((ROWS, NARROW), f32),
        in_specs=[apart] * 7,
        out_specs=whole,
        scratch_shapes=scratch,
        compiler_params=pltpu.CompilerParams(collective_id=0, has_side_effects=True, vmem_limit_bytes=53 << 20),
    )(act, blocks_one, pattern_one, count_one, blocks_two, pattern_two, count_two)


def shards(activations, blocks_one, pattern_one, count_one, blocks_two, pattern_two, count_two):
    total = fused(
        pltpu.with_memory_space_constraint(activations, pltpu.MemorySpace.HBM),
        blocks_one.reshape(SLOTS, BLK, BLK),
        pltpu.with_memory_space_constraint(pattern_one.reshape(1, SLOTS), pltpu.MemorySpace.HBM),
        count_one,
        blocks_two.reshape(SLOTS, BLK, BLK),
        pltpu.with_memory_space_constraint(pattern_two.reshape(1, SLOTS), pltpu.MemorySpace.HBM),
        count_two,
    )
    return jnp.maximum(total + BIAS, 0.0).astype(jnp.bfloat16)


def solution(mesh):
    return jax.shard_map(
        shards,
        mesh=mesh,
        in_specs=(
            P("col", "row"),
            P("row", "col", None, None, None),
            P("row", "col", None),
            P("row", "col"),
            P("col", "row", None, None, None),
            P("col", "row", None),
            P("col", "row"),
        ),
        out_specs=P("col", "row"),
        check_vma=False,
    )
```
